32 devices in a mesh: line: 2 (over y), bin: 16 (over z, x, core).
Axes of the slice: x: 2, y: 2, z: 4, core: 2. Of those that a mesh axis runs over, the one named last changes fastest.
Arguments:
- predicted: bfloat16 [4096, 2048], P(('line', 'bin')), parts along dimension 0, may hold values from -1200 to 1200
- observed: float32 [4096, 2048], P(('line', 'bin')), parts along dimension 0, may hold values from -1200 to 1200
- data_weight: float32 [4096, 2048], P(('line', 'bin')), parts along dimension 0, may hold values from 0.5 to 2
- bin_ids: int32 [4096], P(('line', 'bin')), parts along dimension 0, may hold values from 0 to 31, as said below
- offset_slots: int32 [4096], P(('line', 'bin')), parts along dimension 0, may hold values from 0 to 63, as said below
- conv_in: bfloat16 [3, 3, 48], replicated, may hold values from -2 to 2
- conv_mid: bfloat16 [3, 3, 48, 48], replicated, may hold values from -0.3125 to 0.3125
- conv_out: bfloat16 [3, 3, 48], replicated, may hold values from -0.3125 to 0.3125
Outputs:
- residual_traces: bfloat16 [4096, 2048], P(('line', 'bin')), parts along dimension 0
The draws below stay inside these ranges and needn't reach their ends.
There are 2 independent parts, one for each index of `line`. The reference program is written for one: setup_inputs(seed, part) draws one part's arguments, and reference() takes and returns one part's arrays. A program takes and returns all parts, laid end to end along the dimension named above; an argument that names none is the same for every part. Nothing has to cross between parts.
Inputs may be any that keep to these rules, and one draw needn't show every extreme that they name: `bin_ids`: bin b belongs to index b // 2 of bin. The traces of one device go at most 16 to one owner and at most 8 to one bin, both reached in every draw. Taken by owner index minus the sender's index, modulo the devices of bin, every device sends the same counts. Every owner receives exactly 128 traces, 64 in each of its bins. `offset_slots`: no two traces have the same bin and slot.
All inputs are finite; a program needn't handle non-finite values.
Results may differ from the reference program's by a relative error of at most 0.0065.
Values may be sent and summed in bfloat16 or wider, within the bound.
A program may use at most 256 MiB of HBM per device.

```python
import math
import jax
import jax.numpy as jnp
from jax import lax

NT = 2048
CHAN = 48
OFFS = 64
TR_DEV = 128
TRACES = 2048
BIN_DEV = 2
BINS = 32
CAP = 16


def trace_layout(key):
    owners = TRACES // TR_DEV
    light = max(1, TR_DEV // owners)
    heavy = TR_DEV // (2 * CAP)
    spread = TR_DEV // 2 // light
    base = jax.random.fold_in(key, 11)
    key_order, key_bins, key_slots, key_rows = jax.random.split(base, 4)
    order = jax.random.permutation(key_order, owners).astype(jnp.int32)
    counts = jnp.where(order < heavy, CAP, jnp.where(order < heavy + spread, light, 0)).astype(jnp.int32)
    bounds = jnp.cumsum(counts)
    row_index = jnp.arange(TR_DEV, dtype=jnp.int32)
    distance = jnp.sum((bounds[None, :] <= row_index[:, None]).astype(jnp.int32), axis=1)
    sender = jnp.arange(owners, dtype=jnp.int32)[:, None]
    owner_dev = (sender + distance[None, :]) % owners
    raw_bin = row_index % BIN_DEV
    raw_slot = row_index // BIN_DEV
    bin_perm = jax.vmap(lambda sub_key: jax.random.permutation(sub_key, BIN_DEV))(jax.random.split(key_bins, owners)).astype(jnp.int32)
    scores = jax.random.randint(key_slots, (owners, BIN_DEV, OFFS), 2, 1 << 20) * OFFS + jnp.arange(OFFS, dtype=jnp.int32)
    scores = scores.at[:, :, OFFS - 1].set(0).at[:, :, 0].set(1)
    slot_perm = jnp.argsort(scores, axis=-1).astype(jnp.int32)
    local_bin = bin_perm[owner_dev, raw_bin[None, :]]
    slot_value = slot_perm[owner_dev, raw_bin[None, :], raw_slot[None, :]]
    bin_value = owner_dev * BIN_DEV + local_bin
    row_perm = jax.vmap(lambda sub_key: jax.random.permutation(sub_key, TR_DEV))(jax.random.split(key_rows, owners)).astype(jnp.int32)
    bin_value = jnp.take_along_axis(bin_value, row_perm, axis=1)
    slot_value = jnp.take_along_axis(slot_value, row_perm, axis=1)
    return (bin_value.reshape(-1).astype(jnp.int32), slot_value.reshape(-1).astype(jnp.int32))


def draw_bin_ids(key, part):
    return trace_layout(key)[0]


def draw_offset_slots(key, part):
    return trace_layout(key)[1]


def trace_scales(key):
    key_rows, key_cols = jax.random.split(jax.random.fold_in(key, 21))
    position = jnp.arange(TRACES, dtype=jnp.float32) / TRACES
    top = 10.0
    row_scale = jnp.exp(jax.random.uniform(key_rows, (TRACES,)) * math.log(top)) * (1.0 + 0.75 * position)
    col_scale = jnp.exp(jax.random.uniform(key_cols, (NT,)) * math.log(10.0))
    return (row_scale, col_scale)


def rough_field(key):
    field = jax.random.normal(key, (TRACES, NT))
    return jnp.clip(field, -4.0, 4.0)


def draw_predicted(key, part):
    row_scale, col_scale = trace_scales(key)
    field = rough_field(jax.random.fold_in(key, 31))
    return (field * row_scale[:, None] * col_scale[None, :]).astype(jnp.bfloat16)


def draw_observed(key, part):
    row_scale, col_scale = trace_scales(key)
    field = rough_field(jax.random.fold_in(key, 41))
    return (field * row_scale[:, None] * col_scale[None, :]).astype(jnp.float32)


def block_scale(own_key, extent, shards, smallest, high):
    factor_of, own = 1.0, jax.random.fold_in(own_key, 6)
    for dim, shards_of in shards:
        steps = jnp.exp(jax.random.uniform(jax.random.fold_in(own, dim), (shards_of,), jnp.float32, smallest / len(shards), high / len(shards)))
        factor_of = factor_of * jnp.repeat(steps, extent[dim] // shards_of).reshape([-1 if axis == dim else 1 for axis in range(len(extent))])
    return factor_of


def centred(key, extent, scale, bound, held_as=jnp.bfloat16):
    result = scale * jax.random.normal(key, extent, jnp.float32)
    return jnp.clip(result, min=-bound, max=bound).astype(held_as)


def setup_inputs(seed: int = 0, part: int = 0) -> dict:
    seeds = jax.random.split(jax.random.key(seed), 9)
    own_keys = jax.random.split(jax.random.fold_in(seeds[8], part), 9)
    predicted = draw_predicted(jax.random.fold_in(jax.random.fold_in(seeds[8], part), 71), part)
    observed = draw_observed(jax.random.fold_in(jax.random.fold_in(seeds[8], part), 71), part)
    data_weight = jnp.clip(jnp.exp(math.log(2.0) - 1.3862944 * jax.random.uniform(own_keys[2], (TRACES, NT), jnp.float32) ** block_scale(own_keys[2], (TRACES, NT), ((0, 16),), -0.2, 0.2)), 0.5, 2.0)
    bin_ids = draw_bin_ids(jax.random.fold_in(jax.random.fold_in(seeds[8], part), 71), part)
    offset_slots = draw_offset_slots(jax.random.fold_in(jax.random.fold_in(seeds[8], part), 71), part)
    conv_in = centred(seeds[5], (3, 3, CHAN), 9 ** -0.5, 2.0)
    conv_mid = centred(seeds[6], (3, 3, CHAN, CHAN), (9 * CHAN) ** -0.5, 0.3125)
    conv_out = centred(seeds[7], (3, 3, CHAN), (9 * CHAN) ** -0.5, 0.3125)
    return {"predicted": predicted, "observed": observed, "data_weight": data_weight, "bin_ids": bin_ids, "offset_slots": offset_slots, "conv_in": conv_in, "conv_mid": conv_mid, "conv_out": conv_out}


def shifted(values, along_offset, along_time):
    last = values.ndim - 1
    span_x = values.shape[-2]
    span_t = values.shape[-1]
    pad_x = abs(along_offset)
    pad_t = abs(along_time)
    widths = [(0, 0)] * (values.ndim - 2) + [(pad_x, pad_x), (pad_t, pad_t)]
    padded = jnp.pad(values, widths)
    padded = lax.slice_in_dim(padded, pad_x + along_offset, pad_x + along_offset + span_x, axis=last - 1)
    return lax.slice_in_dim(padded, pad_t + along_time, pad_t + along_time + span_t, axis=last)

def network(panel, conv_in, conv_mid, conv_out):
    values = panel.astype(jnp.float32)
    first_sum = jnp.zeros((CHAN,) + values.shape, jnp.float32)
    for row_tap in range(3):
        for time_tap in range(3):
            weights = conv_in[row_tap, time_tap].astype(jnp.float32)
            first_sum = first_sum + weights[:, None, None] * shifted(values, row_tap - 1, time_tap - 1)[None]
    first_hidden = jax.nn.silu(first_sum).astype(jnp.bfloat16)
    first_wide = first_hidden.astype(jnp.float32)
    second_sum = jnp.zeros((CHAN,) + values.shape, jnp.float32)
    for row_tap in range(3):
        for time_tap in range(3):
            second_sum = second_sum + jnp.einsum('io,ixt->oxt', conv_mid[row_tap, time_tap].astype(jnp.float32), shifted(first_wide, 2 * (row_tap - 1), 4 * (time_tap - 1)), precision=lax.Precision.HIGHEST)
    second_hidden = (first_wide + jax.nn.silu(second_sum)).astype(jnp.bfloat16)
    second_wide = second_hidden.astype(jnp.float32)
    third_sum = jnp.zeros(values.shape, jnp.float32)
    for row_tap in range(3):
        for time_tap in range(3):
            third_sum = third_sum + jnp.einsum('i,ixt->xt', conv_out[row_tap, time_tap].astype(jnp.float32), shifted(second_wide, row_tap - 1, time_tap - 1), precision=lax.Precision.HIGHEST)
    return (values + third_sum).astype(jnp.bfloat16)

def reference(predicted, observed, data_weight, bin_ids, offset_slots, conv_in, conv_mid, conv_out):
    panel_cell = (bin_ids * OFFS + offset_slots).astype(jnp.int32)
    panels = jnp.zeros((BINS * OFFS, NT), jnp.bfloat16).at[panel_cell].set(predicted).reshape(BINS, OFFS, NT)
    filtered = lax.map(lambda panel: network(panel, conv_in, conv_mid, conv_out), panels)
    gathered = filtered.reshape(BINS * OFFS, NT)[panel_cell]
    misfit = data_weight * (gathered.astype(jnp.float32) - observed)
    mean_square = jnp.mean(misfit * misfit)
    return (misfit * lax.rsqrt(mean_square + 1e-05)).astype(jnp.bfloat16)
```

```python
import jax
import jax.numpy as jnp
from jax import lax
from jax.experimental import pallas as pl
from jax.experimental.pallas import tpu as pltpu
from jax.sharding import PartitionSpec as P

OFFS = 64
CHAN = 48
SEGS = 16
MOST = 46
HALF = (OFFS // 2) * CHAN
WIDE = HALF + 256
TILE = 256
CUTS = (7,)


def kernel_body(
    span,
    chunk_a,
    chunk_b,
    panel_ref,
    w_in_ref,
    w_mid0_ref,
    w_mid1_ref,
    w_mid2_ref,
    w_out_ref,
    out_ref,
    ext_ref,
    p3_ref,
    h1_ref,
    z_ref,
):
    w_mid_refs = (w_mid0_ref, w_mid1_ref, w_mid2_ref)
    blk = SEGS
    n_first = (span + 10) * blk
    n_second = (span + 2) * blk
    tiles = HALF // TILE
    zero_cols = jnp.zeros((n_first, 128), jnp.bfloat16)
    for seg in range(SEGS):
        ext_ref[pl.ds(6 * blk + seg, span, stride=blk), :] = panel_ref[
            pl.ds(seg * span, span), :
        ].astype(jnp.float32)
    edge = jnp.zeros((1, OFFS), jnp.float32)
    for b in range(6):
        ext_ref[pl.ds(b * blk, 1), :] = edge
        ext_ref[pl.ds(b * blk + 1, blk - 1), :] = ext_ref[pl.ds((b + span) * blk, blk - 1), :]
        last = (span + 6 + b) * blk
        ext_ref[pl.ds(last, blk - 1), :] = ext_ref[pl.ds((6 + b) * blk + 1, blk - 1), :]
        ext_ref[pl.ds(last + blk - 1, 1), :] = edge
    for tap in range(3):
        p3_ref[:, pl.ds(tap * OFFS, OFFS)] = ext_ref[pl.ds(tap * blk, n_first), :].astype(
            jnp.bfloat16
        )
    for parity in range(2):
        h1_ref[:, pl.ds(parity * WIDE, 128)] = zero_cols
        h1_ref[:, pl.ds(parity * WIDE + 128 + HALF, 128)] = zero_cols

    @pl.loop(0, n_first // chunk_a)
    def _(step):
        rows = pl.ds(pl.multiple_of(step * chunk_a, 16), chunk_a)
        window = p3_ref[rows, :]
        for parity in range(2):
            for tile in range(tiles):
                half = jnp.dot(
                    window,
                    w_in_ref[:, pl.ds(parity * HALF + tile * TILE, TILE)],
                    preferred_element_type=jnp.float32,
                )
                h1_ref[rows, pl.ds(parity * WIDE + 128 + tile * TILE, TILE)] = (
                    half + half * jnp.tanh(half)
                ).astype(jnp.bfloat16)

    seg = lax.broadcasted_iota(jnp.int32, (blk, 1), 0)
    for b in range(5):
        head = pl.ds(b * blk, blk)
        h1_ref[head, :] = jnp.where(seg == 0, 0.0, h1_ref[head, :].astype(jnp.float32)).astype(
            jnp.bfloat16
        )
        tail = pl.ds((span + 5 + b) * blk, blk)
        h1_ref[tail, :] = jnp.where(
            seg == SEGS - 1, 0.0, h1_ref[tail, :].astype(jnp.float32)
        ).astype(jnp.bfloat16)

    @pl.loop(0, n_second // chunk_b)
    def _(step):
        base = pl.multiple_of(step * chunk_b, 16)
        total = jnp.zeros((chunk_b, 3 * OFFS), jnp.float32)
        for parity in range(2):
            for tile in range(tiles):
                half = jnp.zeros((chunk_b, TILE), jnp.float32)
                for tap in range(3):
                    half = half + jnp.dot(
                        h1_ref[
                            pl.ds(base + 4 * blk * tap, chunk_b),
                            pl.ds(parity * WIDE + tile * TILE, 512),
                        ],
                        w_mid_refs[tile % 3][pl.ds(tap * 512, 512), :],
                        preferred_element_type=jnp.float32,
                    )
                first = h1_ref[
                    pl.ds(base + 4 * blk, chunk_b),
                    pl.ds(parity * WIDE + 128 + tile * TILE, TILE),
                ].astype(jnp.float32)
                second = (first + (half + half * jnp.tanh(half))).astype(jnp.bfloat16)
                total = total + jnp.dot(
                    second,
                    w_out_ref[pl.ds(parity * HALF + tile * TILE, TILE), :],
                    preferred_element_type=jnp.float32,
                )
        z_ref[pl.ds(base, chunk_b), :] = total

    z_ref[pl.ds(0, blk), :] = jnp.where(seg == 0, 0.0, z_ref[pl.ds(0, blk), :])
    last = pl.ds((span + 1) * blk, blk)
    z_ref[last, :] = jnp.where(seg == SEGS - 1, 0.0, z_ref[last, :])

    n_out = span * blk

    @pl.loop(0, 8)
    def _(step):
        size = n_out // 8
        base = pl.multiple_of(step * size, 16)
        left = z_ref[pl.ds(base, size), :][:, 0:OFFS]
        mid = z_ref[pl.ds(base + blk, size), :][:, OFFS : 2 * OFFS]
        right = z_ref[pl.ds(base + 2 * blk, size), :][:, 2 * OFFS : 3 * OFFS]
        centre = p3_ref[pl.ds(base + 5 * blk, size), :].astype(jnp.float32)[:, OFFS : 2 * OFFS]
        ext_ref[pl.ds(base, size), :] = centre + (left + mid + right)

    for seg in range(SEGS):
        out_ref[pl.ds(seg * span, span), :] = ext_ref[
            pl.ds(seg, span, stride=blk), :
        ].astype(jnp.bfloat16)


def largest_chunk(blocks, most):
    return max(d for d in range(1, most + 1) if blocks % d == 0)


def by_chan(v):
    return (v * 43691) >> 21


def one_hot(remainder, index, value):
    return jnp.where(remainder == index, value, 0.0).astype(jnp.bfloat16)


def weights_body(
    conv_in_ref,
    conv_mid_ref,
    conv_out_ref,
    w_in_ref,
    w_mid0_ref,
    w_mid1_ref,
    w_mid2_ref,
    w_out_ref,
):
    f32 = jnp.float32

    def iota(shape, axis):
        return lax.broadcasted_iota(jnp.int32, shape, axis)

    def offset_of(place):
        return jnp.where(place < OFFS // 2, 2 * place, 2 * place - OFFS + 1)

    others = iota((OFFS, 1), 0) + 1

    @pl.loop(0, 6)
    def _(part):
        base = pl.multiple_of(part * 512, 512)
        lane = iota((1, 512), 1) + base
        place = by_chan(lane)
        near = others - offset_of(place)
        spread = one_hot(lane - CHAN * place, iota((CHAN, 1), 0), 0.5)
        wide = [jnp.dot(conv_in_ref[a], spread, preferred_element_type=f32) for a in range(3)]
        for d in range(3):
            value = jnp.zeros((OFFS, 512), f32)
            for a in range(3):
                value = jnp.where(near == a, wide[a][d : d + 1, :], value)
            w_in_ref[pl.ds(d * OFFS, OFFS), pl.ds(base, 512)] = value.astype(jnp.bfloat16)

    for m, w_mid_ref in enumerate((w_mid0_ref, w_mid1_ref, w_mid2_ref)):
        x = iota((512, 1), 0) + (256 * m - 128 + 3 * CHAN)
        y = iota((1, TILE), 1) + 256 * m
        cell_x = by_chan(x)
        cell_y = by_chan(y)
        rows = one_hot(x - CHAN * cell_x, iota((1, CHAN), 1), 1.0)
        cols = one_hot(y - CHAN * cell_y, iota((CHAN, 1), 0), 0.5)
        wide = jnp.dot(conv_mid_ref[...], cols, preferred_element_type=f32)
        wide = wide.astype(jnp.bfloat16)
        tap = cell_x - 2 - cell_y
        for d in range(3):
            value = jnp.zeros((512, TILE), f32)
            for a in range(3):
                start = (a * 3 + d) * CHAN
                part = jnp.dot(
                    rows, wide[start : start + CHAN, :], preferred_element_type=f32
                )
                value = jnp.where(tap == a, part, value)
            w_mid_ref[pl.ds(d * 512, 512), :] = value.astype(jnp.bfloat16)

    triple = iota((1, 3 * OFFS), 1)
    group = triple // OFFS
    wide_out = []
    for a in range(3):
        value = jnp.zeros((CHAN, 3 * OFFS), f32)
        for d in range(3):
            value = jnp.where(group == d, conv_out_ref[a, :, d : d + 1].astype(f32), value)
        wide_out.append(value.astype(jnp.bfloat16))

    @pl.loop(0, 6)
    def _(part):
        base = pl.multiple_of(part * 512, 512)
        lane = iota((512, 1), 0) + base
        place = by_chan(lane)
        near = offset_of(place) + 1 - (triple - OFFS * group)
        across = one_hot(lane - CHAN * place, iota((1, CHAN), 1), 1.0)
        value = jnp.zeros((512, 3 * OFFS), f32)
        for a in range(3):
            value = jnp.where(
                near == a, jnp.dot(across, wide_out[a], preferred_element_type=f32), value
            )
        w_out_ref[pl.ds(base, 512), :] = value.astype(jnp.bfloat16)


def band_weights(conv_in, conv_mid, conv_out):
    bf16 = jnp.bfloat16
    mid = jax.ShapeDtypeStruct((1536, TILE), bf16)
    return pl.pallas_call(
        weights_body,
        out_shape=(
            jax.ShapeDtypeStruct((3 * OFFS, OFFS * CHAN), bf16),
            mid,
            mid,
            mid,
            jax.ShapeDtypeStruct((OFFS * CHAN, 3 * OFFS), bf16),
        ),
        in_specs=[pl.BlockSpec(memory_space=pltpu.VMEM)] * 3,
        out_specs=[pl.BlockSpec(memory_space=pltpu.VMEM)] * 5,
        compiler_params=pltpu.CompilerParams(vmem_limit_bytes=40 * 1024 * 1024),
        name="band_weights",
    )(conv_in, conv_mid.reshape(9 * CHAN, CHAN), conv_out.transpose(0, 2, 1))


def filter_rows(panel, weights):
    samples, offs = panel.shape
    span = samples // SEGS
    blk = SEGS
    chunk_a = largest_chunk(span + 10, MOST) * blk
    chunk_b = largest_chunk(span + 2, MOST) * blk

    def body(*refs):
        kernel_body(span, chunk_a, chunk_b, *refs)

    return pl.pallas_call(
        body,
        out_shape=jax.ShapeDtypeStruct((span * blk, offs), jnp.bfloat16),
        in_specs=[pl.BlockSpec(memory_space=pltpu.VMEM)] * 6,
        out_specs=pl.BlockSpec(memory_space=pltpu.VMEM),
        scratch_shapes=[
            pltpu.VMEM(((span + 12) * blk, offs), jnp.float32),
            pltpu.VMEM(((span + 10) * blk, 3 * offs), jnp.bfloat16),
            pltpu.VMEM(((span + 10) * blk, 2 * WIDE), jnp.bfloat16),
            pltpu.VMEM(((span + 2) * blk, 3 * offs), jnp.float32),
        ],
        compiler_params=pltpu.CompilerParams(vmem_limit_bytes=48 * 1024 * 1024),
        name="panel_filter",
    )(panel, *weights)


def by_ops(predicted, observed, data_weight, bin_ids, offset_slots, conv_in, conv_mid, conv_out):
    tr_dev, samples = predicted.shape
    owners = lax.axis_size("bin")
    bin_dev = tr_dev // OFFS
    capacity = max(1, tr_dev // owners)
    slots = owners * capacity
    row_index = jnp.arange(tr_dev, dtype=jnp.int32)
    earlier = row_index[None, :] < row_index[:, None]
    same_bin = bin_ids[:, None] == bin_ids[None, :]
    position = jnp.sum((same_bin & earlier).astype(jnp.int32), axis=1)
    owner_slot = (bin_ids // bin_dev) * capacity + position
    local_bin = bin_ids % bin_dev
    mark = jnp.broadcast_to((offset_slots + 1).astype(jnp.bfloat16)[:, None], (tr_dev, 128))
    labelled = jnp.concatenate([predicted, mark], axis=1)
    slot_index = jnp.arange(slots, dtype=jnp.int32)
    offsets = jnp.arange(OFFS, dtype=jnp.int32)

    picks = []
    arrivals = []
    for b in range(bin_dev):
        send_slot = jnp.where(local_bin == b, owner_slot, -1)
        pick = (slot_index[:, None] == send_slot[None, :]).astype(jnp.bfloat16)
        outgoing = jnp.dot(pick, labelled, preferred_element_type=jnp.float32)
        outgoing = outgoing.astype(jnp.bfloat16).reshape(owners, capacity, samples + 128)
        if b == 0:
            outgoing, conv_in, conv_mid, conv_out = lax.optimization_barrier(
                (outgoing, conv_in, conv_mid, conv_out)
            )
            weights = band_weights(conv_in, conv_mid, conv_out)
        else:
            outgoing, weights = lax.optimization_barrier((outgoing, weights))
        arrived = lax.all_to_all(outgoing, "bin", split_axis=0, concat_axis=0, tiled=True)
        picks.append(pick)
        arrivals.append(arrived.reshape(slots, samples + 128))

    own_rows = 0.0
    for b in range(bin_dev):
        cell = arrivals[b][:, samples].astype(jnp.int32) - 1
        cell_pick = (cell[:, None] == offsets[None, :]).astype(jnp.bfloat16)
        panel = jnp.einsum(
            "sc,st->tc",
            cell_pick,
            arrivals[b][:, :samples],
            preferred_element_type=jnp.float32,
        ).astype(jnp.bfloat16)
        filtered = filter_rows(panel, weights)
        answer = jnp.einsum("sc,tc->st", cell_pick, filtered, preferred_element_type=jnp.float32)
        answer = answer.astype(jnp.bfloat16).reshape(owners, capacity, samples)
        returned = lax.all_to_all(answer, "bin", split_axis=0, concat_axis=0, tiled=True)
        own_rows = own_rows + jnp.einsum(
            "sr,st->rt",
            picks[b],
            returned.reshape(slots, samples),
            preferred_element_type=jnp.float32,
        )
    misfit = data_weight * (own_rows - observed)
    share = jnp.broadcast_to(jnp.sum(misfit * misfit), (owners, 1, 128))
    shares = lax.all_to_all(share, "bin", split_axis=0, concat_axis=0, tiled=True)
    misfit_total = jnp.sum(shares[:, 0, 0])
    mean_square = misfit_total / (tr_dev * owners * samples)
    return (misfit * lax.rsqrt(mean_square + 1e-05)).astype(jnp.bfloat16)


def gathered_pieces(samples):
    cuts = [0] + [samples * part // 16 for part in CUTS] + [samples]
    return list(zip(cuts[:-1], cuts[1:]))


def span_of(piece):
    return (piece[1] - piece[0]) // SEGS


def fused_body(
    owners,
    pred_ref,
    bins_ref,
    offs_ref,
    observed_ref,
    data_weight_ref,
    conv_in_ref,
    conv_mid_ref,
    conv_out_ref,
    out_ref,
    w_in_ref,
    w_mid0_ref,
    w_mid1_ref,
    w_mid2_ref,
    w_out_ref,
    mark_out_ref,
    mark_in_ref,
    outgoing_ref,
    arrived_ref,
    answer_ref,
    returned_ref,
    seen_ref,
    scale_ref,
    misfit_ref,
    natural_ref,
    ext_ref,
    p3_ref,
    h1_ref,
    z_ref,
    back_ref,
    part_ref,
    parts_ref,
    load_sem,
    mark_send,
    mark_recv,
    out_send,
    out_recv,
    back_send,
    back_recv,
    part_send,
    part_recv,
):
    f32 = jnp.float32
    bf16 = jnp.bfloat16
    traces, samples = pred_ref.shape
    group = traces // OFFS * (traces // owners)
    slots = owners * group
    per_bin = traces // owners
    pieces = gathered_pieces(samples)
    me = lax.axis_index("bin")
    w_mid_refs = (w_mid0_ref, w_mid1_ref, w_mid2_ref)

    def partner(step):
        return lax.rem(me + step, owners)

    def rows_of(index, size):
        return pl.ds(pl.multiple_of(index * size, size), size)

    def copy_to(step, source, target, size, lanes, sent, got):
        to = partner(step)
        return pltpu.make_async_remote_copy(
            src_ref=source.at[rows_of(to, size), lanes],
            dst_ref=target.at[rows_of(me, size), lanes],
            send_sem=sent.at[to],
            recv_sem=got.at[me],
            device_id={"bin": to},
            device_id_type=pl.DeviceIdType.MESH,
        )

    def copy_from(step, source, target, size, lanes, sent, got):
        other = partner(step)
        return pltpu.make_async_remote_copy(
            src_ref=source.at[rows_of(other, size), lanes],
            dst_ref=target.at[rows_of(other, size), lanes],
            send_sem=sent.at[other],
            recv_sem=got.at[other],
            device_id={"bin": other},
            device_id_type=pl.DeviceIdType.MESH,
        )

    def start(*what):
        @pl.loop(1, owners)
        def _(step):
            copy_to(step, *what).start()

    def wait_recv(*what):
        @pl.loop(1, owners)
        def _(step):
            copy_from(step, *what).wait_recv()

    def wait_send(*what):
        @pl.loop(1, owners)
        def _(step):
            copy_to(step, *what).wait_send()

    loads = [
        pltpu.make_async_copy(observed_ref, seen_ref, load_sem.at[0]),
        pltpu.make_async_copy(data_weight_ref, scale_ref, load_sem.at[1]),
    ]
    for load in loads:
        load.start()

    barrier = pltpu.get_barrier_semaphore()

    @pl.loop(1, owners)
    def _(step):
        pl.semaphore_signal(
            barrier, inc=1, device_id={"bin": partner(step)}, device_id_type=pl.DeviceIdType.MESH
        )

    def iota(shape, axis):
        return lax.broadcasted_iota(jnp.int32, shape, axis)

    wide = jnp.broadcast_to(bins_ref[...], (traces, traces)).astype(f32)
    tall = wide.T
    same = wide == tall
    above = iota((traces, traces), 0)
    beside = iota((traces, traces), 1)
    slot_row = wide[0:1, :] * per_bin + jnp.sum(
        jnp.where(same & (above < beside), 1.0, 0.0), axis=0, keepdims=True
    )
    slot_col = tall[:, 0:1] * per_bin + jnp.sum(
        jnp.where(same & (beside < above), 1.0, 0.0), axis=1, keepdims=True
    )
    pick = jnp.where(iota((slots, 1), 0).astype(f32) == slot_row, 1.0, 0.0).astype(bf16)
    pick_back = jnp.where(slot_col == iota((1, slots), 1).astype(f32), 1.0, 0.0).astype(bf16)
    mark = jnp.broadcast_to(offs_ref[...] + 1, (traces, traces)).astype(f32).T.astype(bf16)
    mark_out_ref[...] = jnp.dot(pick, mark, preferred_element_type=f32).astype(bf16)

    all_marks = (mark_out_ref, mark_in_ref, group, pl.ds(0, traces), mark_send, mark_recv)

    def forward(index):
        low = 0 if index == 0 else pieces[index][0] + 128
        high = samples if index == len(pieces) - 1 else pieces[index][1] + 128
        return low, high

    def forward_copy(index):
        low, high = forward(index)
        return (
            outgoing_ref,
            arrived_ref,
            group,
            pl.ds(low, high - low),
            out_send.at[index],
            out_recv.at[index],
        )

    def back_copy(index):
        low, high = pieces[index]
        return (
            answer_ref,
            returned_ref,
            group,
            pl.ds(low, high - low),
            back_send.at[index],
            back_recv.at[index],
        )

    def fill(index):
        low, high = forward(index)
        for lane in range(low, high, 128):
            outgoing_ref[:, pl.ds(lane, 128)] = jnp.dot(
                pick, pred_ref[:, pl.ds(lane, 128)], preferred_element_type=f32
            ).astype(bf16)

    mine = rows_of(me, group)
    fill(0)
    pl.semaphore_wait(barrier, owners - 1)
    start(*all_marks)
    start(*forward_copy(0))
    for index in range(1, len(pieces)):
        fill(index)
        start(*forward_copy(index))
    mark_in_ref[mine, :] = mark_out_ref[mine, :]
    arrived_ref[mine, :] = outgoing_ref[mine, :]
    weights_body(
        conv_in_ref,
        conv_mid_ref,
        conv_out_ref,
        w_in_ref,
        w_mid0_ref,
        w_mid1_ref,
        w_mid2_ref,
        w_out_ref,
    )
    cells = 2 * OFFS
    nothing = jnp.zeros((8, cells), f32)
    natural_ref[pl.ds(0, 8), :] = nothing
    natural_ref[pl.ds(samples + 8, 8), :] = nothing
    for parity in range(2):
        zero_cols = jnp.zeros((h1_ref.shape[0], 128), bf16)
        h1_ref[:, pl.ds(parity * WIDE, 128)] = zero_cols
        h1_ref[:, pl.ds(parity * WIDE + 128 + HALF, 128)] = zero_cols

    wait_recv(*all_marks)
    cell = iota((slots, cells), 1)
    row = iota((slots, cells), 0)
    offset = (cell & (OFFS - 1)) + 1
    bin_of_row = lax.rem(row, group) >= per_bin
    bin_of_cell = cell >= OFFS
    hit = (mark_in_ref[...].astype(f32) == offset.astype(f32)) & (bin_of_row == bin_of_cell)
    cell_pick_wide = jnp.where(hit, 1.0, 0.0)
    cell_pick = cell_pick_wide.astype(bf16)
    cell_pick_back = cell_pick_wide.T.astype(bf16)

    blk = SEGS
    tiles = HALF // TILE
    seg_index = iota((blk, 1), 0)

    def mask_rows(ref, first_row, edge):
        rows = pl.ds(first_row, blk)
        ref[rows, :] = jnp.where(seg_index == edge, 0.0, ref[rows, :].astype(f32)).astype(
            ref.dtype
        )

    total = jnp.zeros((8, 128), f32)
    for index, piece in enumerate(pieces):
        span = span_of(piece)
        at_start = index == 0
        at_end = index == len(pieces) - 1
        n_first = (span + 10) * blk
        n_second = (span + 2) * blk
        n_out = span * blk
        chunk_a = largest_chunk(span + 10, MOST) * blk
        chunk_b = largest_chunk(span + 2, MOST) * blk
        wait_recv(*forward_copy(index))
        for lane in range(*forward(index), 128):
            natural_ref[pl.ds(8 + lane, 128), :] = jnp.dot(
                cell_pick_back, arrived_ref[:, pl.ds(lane, 128)], preferred_element_type=f32
            ).T
        for seg in range(SEGS):
            ext_ref[pl.ds(seg, span + 12, stride=blk), :] = natural_ref[
                pl.ds(piece[0] + seg * span + 2, span + 12), :
            ]
        for which in range(2):
            for tap in range(3):
                p3_ref[which, pl.ds(0, n_first), pl.ds(tap * OFFS, OFFS)] = ext_ref[
                    pl.ds(tap * blk, n_first), :
                ][:, which * OFFS : (which + 1) * OFFS].astype(bf16)

        @pl.loop(0, 2)
        def _(which):
            @pl.loop(0, n_first // chunk_a)
            def _(step):
                rows = pl.ds(pl.multiple_of(step * chunk_a, 16), chunk_a)
                window = p3_ref[which, rows, :]
                for parity in range(2):
                    for tile in range(tiles):
                        half = jnp.dot(
                            window,
                            w_in_ref[:, pl.ds(parity * HALF + tile * TILE, TILE)],
                            preferred_element_type=f32,
                        )
                        h1_ref[rows, pl.ds(parity * WIDE + 128 + tile * TILE, TILE)] = (
                            half + half * jnp.tanh(half)
                        ).astype(bf16)

            for b in range(5):
                if at_start:
                    mask_rows(h1_ref, b * blk, 0)
                if at_end:
                    mask_rows(h1_ref, (span + 5 + b) * blk, SEGS - 1)

            @pl.loop(0, n_second // chunk_b)
            def _(step):
                base = pl.multiple_of(step * chunk_b, 16)
                acc = jnp.zeros((chunk_b, 3 * OFFS), f32)
                for parity in range(2):
                    for tile in range(tiles):
                        half = jnp.zeros((chunk_b, TILE), f32)
                        for tap in range(3):
                            half = half + jnp.dot(
                                h1_ref[
                                    pl.ds(base + 4 * blk * tap, chunk_b),
                                    pl.ds(parity * WIDE + tile * TILE, 512),
                                ],
                                w_mid_refs[tile % 3][pl.ds(tap * 512, 512), :],
                                preferred_element_type=f32,
                            )
                        first = h1_ref[
                            pl.ds(base + 4 * blk, chunk_b),
                            pl.ds(parity * WIDE + 128 + tile * TILE, TILE),
                        ].astype(f32)
                        second = (first + (half + half * jnp.tanh(half))).astype(bf16)
                        acc = acc + jnp.dot(
                            second,
                            w_out_ref[pl.ds(parity * HALF + tile * TILE, TILE), :],
                            preferred_element_type=f32,
                        )
                z_ref[which, pl.ds(base, chunk_b), :] = acc

        for which in range(2):
            if at_start:
                mask_rows(z_ref.at[which], 0, 0)
            if at_end:
                mask_rows(z_ref.at[which], (span + 1) * blk, SEGS - 1)

        @pl.loop(0, 8)
        def _(step):
            size = n_out // 8
            base = pl.multiple_of(step * size, 16)
            sums = []
            for which in range(2):
                left = z_ref[which, pl.ds(base, size), :][:, 0:OFFS]
                mid = z_ref[which, pl.ds(base + blk, size), :][:, OFFS : 2 * OFFS]
                right = z_ref[which, pl.ds(base + 2 * blk, size), :][:, 2 * OFFS : 3 * OFFS]
                sums.append(left + mid + right)
            centre = ext_ref[pl.ds(base + 6 * blk, size), :]
            ext_ref[pl.ds(base, size), :] = centre + jnp.concatenate(sums, axis=1)

        for seg in range(SEGS):
            back_ref[pl.ds(seg * span, span), :] = ext_ref[pl.ds(seg, span, stride=blk), :]
        for lane in range(0, n_out, 128):
            answer_ref[:, pl.ds(piece[0] + lane, 128)] = jnp.dot(
                cell_pick,
                back_ref[pl.ds(lane, 128), :].T.astype(bf16),
                preferred_element_type=f32,
            ).astype(bf16)
        start(*back_copy(index))

    returned_ref[mine, :] = answer_ref[mine, :]
    for load in loads:
        load.wait()
    for index, piece in enumerate(pieces):
        wait_recv(*back_copy(index))
        for lane in range(*piece, 128):
            lanes = pl.ds(lane, 128)
            own = jnp.dot(pick_back, returned_ref[:, lanes], preferred_element_type=f32)
            miss = scale_ref[:, lanes] * (own - seen_ref[:, lanes])
            misfit_ref[:, lanes] = miss
            total = total + jnp.sum((miss * miss).reshape(traces // 8, 8, 128), axis=0)

    part_ref[...] = total

    def part_copy(step, here):
        other = partner(step)
        return pltpu.make_async_remote_copy(
            src_ref=part_ref,
            dst_ref=parts_ref.at[rows_of(me if here else other, 8), :],
            send_sem=part_send.at[other],
            recv_sem=part_recv.at[me if here else other],
            device_id={"bin": other},
            device_id_type=pl.DeviceIdType.MESH,
        )

    @pl.loop(1, owners)
    def _(step):
        part_copy(step, True).start()

    parts_ref[rows_of(me, 8), :] = total

    @pl.loop(1, owners)
    def _(step):
        part_copy(step, False).wait_recv()

    mean_square = jnp.sum(parts_ref[...], keepdims=True) / (traces * owners * samples)
    out_ref[...] = (misfit_ref[...] * lax.rsqrt(mean_square + 1e-05)).astype(bf16)

    @pl.loop(1, owners)
    def _(step):
        part_copy(step, True).wait_send()

    wait_send(*all_marks)
    for index in range(len(pieces)):
        wait_send(*forward_copy(index))
        wait_send(*back_copy(index))


def fused(predicted, observed, data_weight, bin_ids, offset_slots, conv_in, conv_mid, conv_out):
    traces, samples = predicted.shape
    owners = lax.axis_size("bin")
    group = traces // OFFS * (traces // owners)
    slots = owners * group
    pieces = gathered_pieces(samples)
    count = len(pieces)
    span = max(span_of(piece) for piece in pieces)
    cells = 2 * OFFS
    bf16 = jnp.bfloat16
    f32 = jnp.float32
    dma = pltpu.SemaphoreType.DMA
    vmem = pl.BlockSpec(memory_space=pltpu.VMEM)
    anywhere = pl.BlockSpec(memory_space=pl.ANY)

    def body(*refs):
        fused_body(owners, *refs)

    return pl.pallas_call(
        body,
        out_shape=jax.ShapeDtypeStruct((traces, samples), bf16),
        in_specs=[vmem, vmem, vmem, anywhere, anywhere, vmem, vmem, vmem],
        out_specs=vmem,
        scratch_shapes=[
            pltpu.VMEM((3 * OFFS, OFFS * CHAN), bf16),
            pltpu.VMEM((1536, TILE), bf16),
            pltpu.VMEM((1536, TILE), bf16),
            pltpu.VMEM((1536, TILE), bf16),
            pltpu.VMEM((OFFS * CHAN, 3 * OFFS), bf16),
            pltpu.VMEM((slots, traces), bf16),
            pltpu.VMEM((slots, traces), bf16),
            pltpu.VMEM((slots, samples), bf16),
            pltpu.VMEM((slots, samples), bf16),
            pltpu.VMEM((slots, samples), bf16),
            pltpu.VMEM((slots, samples), bf16),
            pltpu.VMEM((traces, samples), f32),
            pltpu.VMEM((traces, samples), f32),
            pltpu.VMEM((traces, samples), f32),
            pltpu.VMEM((samples + 16, cells), f32),
            pltpu.VMEM(((span + 12) * SEGS, cells), f32),
            pltpu.VMEM((2, (span + 10) * SEGS, 3 * OFFS), bf16),
            pltpu.VMEM(((span + 10) * SEGS, 2 * WIDE), bf16),
            pltpu.VMEM((2, (span + 2) * SEGS, 3 * OFFS), f32),
            pltpu.VMEM((span * SEGS, cells), f32),
            pltpu.VMEM((8, 128), f32),
            pltpu.VMEM((8 * owners, 128), f32),
            dma((2,)),
            dma((owners,)),
            dma((owners,)),
            dma((count, owners)),
            dma((count, owners)),
            dma((count, owners)),
            dma((count, owners)),
            dma((owners,)),
            dma((owners,)),
        ],
        compiler_params=pltpu.CompilerParams(
            collective_id=0, has_side_effects=True, vmem_limit_bytes=56 * 1024 * 1024
        ),
        name="exchange_filter",
    )(
        predicted,
        bin_ids.reshape(1, traces),
        offset_slots.reshape(1, traces),
        observed,
        data_weight,
        conv_in,
        conv_mid.reshape(9 * CHAN, CHAN),
        conv_out.transpose(0, 2, 1),
    )


def local(*args):
    traces = args[0].shape[0]
    owners = lax.axis_size("bin")
    if traces // OFFS * (traces // owners) % 16 == 0:
        return fused(*args)
    return by_ops(*args)


def solution(mesh):
    in_specs = (
        P(("line", "bin"), None),
        P(("line", "bin"), None),
        P(("line", "bin"), None),
        P(("line", "bin")),
        P(("line", "bin")),
        P(),
        P(),
        P(),
    )
    out_specs = P(("line", "bin"), None)
    return jax.shard_map(local, mesh=mesh, in_specs=in_specs, out_specs=out_specs, check_vma=False)
```

```python
import jax
import jax.numpy as jnp
from jax import lax
from jax.experimental import pallas as pl
from jax.experimental.pallas import tpu as pltpu
from jax.sharding import PartitionSpec as P

OFFS = 64
CHAN = 48
SEGS = 16
MOST = 46
TILE = 256
CUTS = (4, 12)
CELLS = TILE // CHAN
SPARE = TILE - CELLS * CHAN
TILES = -(-OFFS // CELLS)
SPLIT_TILE = OFFS // 2 // CELLS
SPLIT = OFFS // 2 % CELLS


def kernel_body(
    span,
    chunk_a,
    chunk_b,
    panel_ref,
    w_in_ref,
    w_mid_ref,
    w_out_ref,
    out_ref,
    ext_ref,
    p3_ref,
    h1_ref,
    z_ref,
):
    blk = SEGS
    n_first = (span + 10) * blk
    n_second = (span + 2) * blk
    for seg in range(SEGS):
        ext_ref[pl.ds(6 * blk + seg, span, stride=blk), :] = panel_ref[
            pl.ds(seg * span, span), :
        ].astype(jnp.float32)
    edge = jnp.zeros((1, OFFS), jnp.float32)
    for b in range(6):
        ext_ref[pl.ds(b * blk, 1), :] = edge
        ext_ref[pl.ds(b * blk + 1, blk - 1), :] = ext_ref[pl.ds((b + span) * blk, blk - 1), :]
        last = (span + 6 + b) * blk
        ext_ref[pl.ds(last, blk - 1), :] = ext_ref[pl.ds((6 + b) * blk + 1, blk - 1), :]
        ext_ref[pl.ds(last + blk - 1, 1), :] = edge
    for tap in range(3):
        p3_ref[:, pl.ds(tap * OFFS, OFFS)] = ext_ref[pl.ds(tap * blk, n_first), :].astype(
            jnp.bfloat16
        )
    @pl.loop(0, n_first // chunk_a)
    def _(step):
        rows = pl.ds(pl.multiple_of(step * chunk_a, 16), chunk_a)
        window = p3_ref[rows, :]
        for tile in range(TILES):
            lanes = pl.ds(tile * TILE, TILE)
            half = jnp.dot(window, w_in_ref[:, lanes], preferred_element_type=jnp.float32)
            h1_ref[rows, lanes] = (half + half * jnp.tanh(half)).astype(jnp.bfloat16)

    seg = lax.broadcasted_iota(jnp.int32, (blk, 1), 0)
    for b in range(5):
        head = pl.ds(b * blk, blk)
        h1_ref[head, :] = jnp.where(seg == 0, 0.0, h1_ref[head, :].astype(jnp.float32)).astype(
            jnp.bfloat16
        )
        tail = pl.ds((span + 5 + b) * blk, blk)
        h1_ref[tail, :] = jnp.where(
            seg == SEGS - 1, 0.0, h1_ref[tail, :].astype(jnp.float32)
        ).astype(jnp.bfloat16)

    @pl.loop(0, n_second // chunk_b)
    def _(step):
        base = pl.multiple_of(step * chunk_b, 16)
        total = jnp.zeros((chunk_b, 3 * OFFS), jnp.float32)
        for tile in range(TILES):
            rows, first = middle_rows(h1_ref, base, chunk_b, tile)
            half = jnp.dot(
                rows,
                w_mid_ref[1 if tile == SPLIT_TILE else 0],
                preferred_element_type=jnp.float32,
            )
            second = first.astype(jnp.float32) + (half + half * jnp.tanh(half))
            total = total + jnp.dot(
                second.astype(jnp.bfloat16),
                w_out_ref[pl.ds(tile * TILE, TILE), :],
                preferred_element_type=jnp.float32,
            )
        z_ref[pl.ds(base, chunk_b), :] = total

    z_ref[pl.ds(0, blk), :] = jnp.where(seg == 0, 0.0, z_ref[pl.ds(0, blk), :])
    last = pl.ds((span + 1) * blk, blk)
    z_ref[last, :] = jnp.where(seg == SEGS - 1, 0.0, z_ref[last, :])

    n_out = span * blk

    @pl.loop(0, 8)
    def _(step):
        size = n_out // 8
        base = pl.multiple_of(step * size, 16)
        left = z_ref[pl.ds(base, size), :][:, 0:OFFS]
        mid = z_ref[pl.ds(base + blk, size), :][:, OFFS : 2 * OFFS]
        right = z_ref[pl.ds(base + 2 * blk, size), :][:, 2 * OFFS : 3 * OFFS]
        centre = p3_ref[pl.ds(base + 5 * blk, size), :].astype(jnp.float32)[:, OFFS : 2 * OFFS]
        ext_ref[pl.ds(base, size), :] = centre + (left + mid + right)

    for seg in range(SEGS):
        out_ref[pl.ds(seg * span, span), :] = ext_ref[
            pl.ds(seg, span, stride=blk), :
        ].astype(jnp.bfloat16)


def largest_chunk(blocks, most):
    return max(d for d in range(1, most + 1) if blocks % d == 0)


def by_chan(v):
    return (v * 43691) >> 21


def one_hot(hit, value):
    return jnp.where(hit, value, 0.0).astype(jnp.bfloat16)


def column(conv_out_ref, a, d):
    row = lax.broadcasted_iota(jnp.int32, (CHAN, CHAN), 0)
    lane = lax.broadcasted_iota(jnp.int32, (CHAN, CHAN), 1)
    taps = jnp.where(row == lane, conv_out_ref[a, d : d + 1, :].astype(jnp.float32), 0.0)
    return jnp.sum(taps, axis=1, keepdims=True)


def weights_body(conv_in_ref, conv_mid_ref, conv_out_ref, w_in_ref, w_mid_ref, w_out_ref):
    f32 = jnp.float32

    def iota(shape, axis):
        return lax.broadcasted_iota(jnp.int32, shape, axis)

    def offset_of(place):
        return jnp.where(place < OFFS // 2, 2 * place, 2 * place - OFFS + 1)

    def cell_of(lane):
        cell = by_chan(lane)
        spare = cell >= CELLS
        return jnp.where(spare, -1, cell), jnp.where(spare, lane - CELLS * CHAN, lane - CHAN * cell)

    others = iota((OFFS, 1), 0) + 1
    chan_down = iota((CHAN, 1), 0)
    chan_across = iota((1, CHAN), 1)

    slot_in, chan_in = cell_of(iota((1, TILE), 1))
    spread = one_hot(chan_in == chan_down, 0.5)
    wide_in = [jnp.dot(conv_in_ref[a], spread, preferred_element_type=f32) for a in range(3)]

    @pl.loop(0, TILES)
    def _(tile):
        base = pl.multiple_of(tile * TILE, TILE)
        near = others - offset_of(slot_in + CELLS * tile)
        for d in range(3):
            value = jnp.zeros((OFFS, TILE), f32)
            for a in range(3):
                value = jnp.where(near == a, wide_in[a][d : d + 1, :], value)
            w_in_ref[pl.ds(d * OFFS, OFFS), pl.ds(base, TILE)] = value.astype(jnp.bfloat16)

    y = iota((1, TILE), 1)
    slot_y = by_chan(y)
    spread_y = one_hot((y - CHAN * slot_y == chan_down) & (slot_y < CELLS), 0.5)
    wide = jnp.dot(conv_mid_ref[...], spread_y, preferred_element_type=f32)

    def taps_of(a, d):
        start = (a * 3 + d) * CHAN
        return wide[start : start + CHAN, :]

    x = iota((TILE, 1), 0)
    slot_x, chan_x = cell_of(x)
    pick = one_hot(chan_x == chan_across, 1.0)
    step = slot_x - slot_y + 1
    apart = (slot_x < SPLIT) != (slot_y < SPLIT)
    for d in range(3):
        value = jnp.zeros((TILE, TILE), f32)
        for a in range(3):
            part = jnp.dot(pick, taps_of(a, d).astype(jnp.bfloat16), preferred_element_type=f32)
            value = jnp.where(step == a, part, value)
        w_mid_ref[0, pl.ds(d * TILE, TILE), :] = value.astype(jnp.bfloat16)
        w_mid_ref[1, pl.ds(d * TILE, TILE), :] = jnp.where(
            apart & (slot_x >= 0), 0.0, value
        ).astype(jnp.bfloat16)
    edge = jnp.zeros((TILE, TILE), f32)
    for d, right, left in ((0, 0, 80), (1, 128, 48), (2, 176, 224)):
        from_right = one_hot((x - right == chan_across) & (x < right + CHAN), 1.0)
        from_left = one_hot(
            (x - left + SPARE == chan_across) & (x >= left) & (x < left + CHAN - SPARE), 1.0
        )
        low = jnp.where(slot_y == 0, taps_of(0, d), 0.0).astype(jnp.bfloat16)
        high = jnp.where(slot_y == CELLS - 1, taps_of(2, d), 0.0).astype(jnp.bfloat16)
        edge = edge + jnp.dot(from_right, high, preferred_element_type=f32)
        edge = edge + jnp.dot(from_left, low, preferred_element_type=f32)
    for kind in range(2):
        w_mid_ref[kind, pl.ds(3 * TILE, TILE), :] = edge.astype(jnp.bfloat16)

    triple = iota((1, 3 * OFFS), 1)
    group = triple // OFFS
    wide_out = []
    for a in range(3):
        value = jnp.zeros((CHAN, 3 * OFFS), f32)
        for d in range(3):
            value = jnp.where(group == d, column(conv_out_ref, a, d), value)
        wide_out.append(value.astype(jnp.bfloat16))
    across = one_hot((chan_x == chan_across) & (slot_x >= 0), 1.0)
    parts = [jnp.dot(across, wide_out[a], preferred_element_type=f32) for a in range(3)]

    @pl.loop(0, TILES)
    def _(tile):
        base = pl.multiple_of(tile * TILE, TILE)
        near = offset_of(slot_x + CELLS * tile) + 1 - (triple - OFFS * group)
        value = jnp.zeros((TILE, 3 * OFFS), f32)
        for a in range(3):
            value = jnp.where(near == a, parts[a], value)
        w_out_ref[pl.ds(base, TILE), :] = value.astype(jnp.bfloat16)


def middle_rows(h1_ref, base, chunk, tile):
    lane = lax.broadcasted_iota(jnp.int32, (1, 128), 1)

    def piece(start, width, tap):
        return h1_ref[pl.ds(base + 4 * SEGS * tap, chunk), pl.ds(start, width)]

    after = min(tile + 1, TILES - 1) * TILE
    right = [piece(after, 128, tap) for tap in range(3)]
    if tile == 0:
        left = [jnp.zeros((chunk, 128), jnp.bfloat16)] * 3
        turned = left
    else:
        left = [piece(tile * TILE - 128, 128, tap) for tap in range(3)]
        turned = [None, pltpu.roll(left[1], 96, 1), pltpu.roll(left[2], 16, 1)]
    low = jnp.where(lane < 48, right[0], jnp.where(lane < 80, turned[1], left[0]))
    high = jnp.where(
        lane < 48, right[1], jnp.where(lane < 96, pltpu.roll(right[2], 48, 1), turned[2])
    )
    whole = [piece(tile * TILE, TILE, tap) for tap in range(3)]
    return jnp.concatenate(whole + [low, high], axis=1), whole[1]


def band_weights(conv_in, conv_mid, conv_out):
    bf16 = jnp.bfloat16
    return pl.pallas_call(
        weights_body,
        out_shape=(
            jax.ShapeDtypeStruct((3 * OFFS, TILES * TILE), bf16),
            jax.ShapeDtypeStruct((2, 4 * TILE, TILE), bf16),
            jax.ShapeDtypeStruct((TILES * TILE, 3 * OFFS), bf16),
        ),
        in_specs=[pl.BlockSpec(memory_space=pltpu.VMEM)] * 3,
        out_specs=[pl.BlockSpec(memory_space=pltpu.VMEM)] * 3,
        compiler_params=pltpu.CompilerParams(vmem_limit_bytes=40 * 1024 * 1024),
        name="band_weights",
    )(conv_in, conv_mid.reshape(9 * CHAN, CHAN), conv_out)


def filter_rows(panel, weights):
    samples, offs = panel.shape
    span = samples // SEGS
    blk = SEGS
    chunk_a = largest_chunk(span + 10, MOST) * blk
    chunk_b = largest_chunk(span + 2, MOST) * blk

    def body(*refs):
        kernel_body(span, chunk_a, chunk_b, *refs)

    return pl.pallas_call(
        body,
        out_shape=jax.ShapeDtypeStruct((span * blk, offs), jnp.bfloat16),
        in_specs=[pl.BlockSpec(memory_space=pltpu.VMEM)] * 4,
        out_specs=pl.BlockSpec(memory_space=pltpu.VMEM),
        scratch_shapes=[
            pltpu.VMEM(((span + 12) * blk, offs), jnp.float32),
            pltpu.VMEM(((span + 10) * blk, 3 * offs), jnp.bfloat16),
            pltpu.VMEM(((span + 10) * blk, TILES * TILE), jnp.bfloat16),
            pltpu.VMEM(((span + 2) * blk, 3 * offs), jnp.float32),
        ],
        compiler_params=pltpu.CompilerParams(vmem_limit_bytes=48 * 1024 * 1024),
        name="panel_filter",
    )(panel, *weights)


def by_ops(predicted, observed, data_weight, bin_ids, offset_slots, conv_in, conv_mid, conv_out):
    tr_dev, samples = predicted.shape
    owners = lax.axis_size("bin")
    bin_dev = tr_dev // OFFS
    capacity = max(1, tr_dev // owners)
    slots = owners * capacity
    row_index = jnp.arange(tr_dev, dtype=jnp.int32)
    earlier = row_index[None, :] < row_index[:, None]
    same_bin = bin_ids[:, None] == bin_ids[None, :]
    position = jnp.sum((same_bin & earlier).astype(jnp.int32), axis=1)
    owner_slot = (bin_ids // bin_dev) * capacity + position
    local_bin = bin_ids % bin_dev
    mark = jnp.broadcast_to((offset_slots + 1).astype(jnp.bfloat16)[:, None], (tr_dev, 128))
    labelled = jnp.concatenate([predicted, mark], axis=1)
    slot_index = jnp.arange(slots, dtype=jnp.int32)
    offsets = jnp.arange(OFFS, dtype=jnp.int32)

    picks = []
    arrivals = []
    for b in range(bin_dev):
        send_slot = jnp.where(local_bin == b, owner_slot, -1)
        pick = (slot_index[:, None] == send_slot[None, :]).astype(jnp.bfloat16)
        outgoing = jnp.dot(pick, labelled, preferred_element_type=jnp.float32)
        outgoing = outgoing.astype(jnp.bfloat16).reshape(owners, capacity, samples + 128)
        if b == 0:
            outgoing, conv_in, conv_mid, conv_out = lax.optimization_barrier(
                (outgoing, conv_in, conv_mid, conv_out)
            )
            weights = band_weights(conv_in, conv_mid, conv_out)
        else:
            outgoing, weights = lax.optimization_barrier((outgoing, weights))
        arrived = lax.all_to_all(outgoing, "bin", split_axis=0, concat_axis=0, tiled=True)
        picks.append(pick)
        arrivals.append(arrived.reshape(slots, samples + 128))

    own_rows = 0.0
    for b in range(bin_dev):
        cell = arrivals[b][:, samples].astype(jnp.int32) - 1
        cell_pick = (cell[:, None] == offsets[None, :]).astype(jnp.bfloat16)
        panel = jnp.einsum(
            "sc,st->tc",
            cell_pick,
            arrivals[b][:, :samples],
            preferred_element_type=jnp.float32,
        ).astype(jnp.bfloat16)
        filtered = filter_rows(panel, weights)
        answer = jnp.einsum("sc,tc->st", cell_pick, filtered, preferred_element_type=jnp.float32)
        answer = answer.astype(jnp.bfloat16).reshape(owners, capacity, samples)
        returned = lax.all_to_all(answer, "bin", split_axis=0, concat_axis=0, tiled=True)
        own_rows = own_rows + jnp.einsum(
            "sr,st->rt",
            picks[b],
            returned.reshape(slots, samples),
            preferred_element_type=jnp.float32,
        )
    misfit = data_weight * (own_rows - observed)
    share = jnp.broadcast_to(jnp.sum(misfit * misfit), (owners, 1, 128))
    shares = lax.all_to_all(share, "bin", split_axis=0, concat_axis=0, tiled=True)
    misfit_total = jnp.sum(shares[:, 0, 0])
    mean_square = misfit_total / (tr_dev * owners * samples)
    return (misfit * lax.rsqrt(mean_square + 1e-05)).astype(jnp.bfloat16)


def gathered_pieces(samples):
    cuts = [0] + [samples * part // 16 for part in CUTS] + [samples]
    return list(zip(cuts[:-1], cuts[1:]))


def span_of(piece):
    return (piece[1] - piece[0]) // SEGS


def fused_body(
    owners,
    pred_ref,
    bins_ref,
    offs_ref,
    observed_ref,
    data_weight_ref,
    conv_in_ref,
    conv_mid_ref,
    conv_out_ref,
    misfit_ref,
    factor_ref,
    w_in_ref,
    w_mid_ref,
    w_out_ref,
    mark_out_ref,
    mark_in_ref,
    outgoing_ref,
    arrived_ref,
    answer_ref,
    returned_ref,
    seen_ref,
    scale_ref,
    natural_ref,
    ext_ref,
    p3_ref,
    h1_ref,
    z_ref,
    back_ref,
    part_ref,
    parts_ref,
    load_sem,
    mark_send,
    mark_recv,
    out_send,
    out_recv,
    back_send,
    back_recv,
    part_send,
    part_recv,
):
    f32 = jnp.float32
    bf16 = jnp.bfloat16
    traces, samples = pred_ref.shape
    group = traces // OFFS * (traces // owners)
    slots = owners * group
    per_bin = traces // owners
    pieces = gathered_pieces(samples)
    me = lax.axis_index("bin")

    def partner(step):
        return lax.rem(me + step, owners)

    def rows_of(index, size):
        return pl.ds(pl.multiple_of(index * size, size), size)

    def copy_to(step, source, target, size, lanes, sent, got):
        to = partner(step)
        return pltpu.make_async_remote_copy(
            src_ref=source.at[rows_of(to, size), lanes],
            dst_ref=target.at[rows_of(me, size), lanes],
            send_sem=sent.at[to],
            recv_sem=got.at[me],
            device_id={"bin": to},
            device_id_type=pl.DeviceIdType.MESH,
        )

    def copy_from(step, source, target, size, lanes, sent, got):
        other = partner(step)
        return pltpu.make_async_remote_copy(
            src_ref=source.at[rows_of(other, size), lanes],
            dst_ref=target.at[rows_of(other, size), lanes],
            send_sem=sent.at[other],
            recv_sem=got.at[other],
            device_id={"bin": other},
            device_id_type=pl.DeviceIdType.MESH,
        )

    def start(*what):
        @pl.loop(1, owners)
        def _(step):
            copy_to(step, *what).start()

    def wait_recv(*what):
        @pl.loop(1, owners)
        def _(step):
            copy_from(step, *what).wait_recv()

    def wait_send(*what):
        @pl.loop(1, owners)
        def _(step):
            copy_to(step, *what).wait_send()

    loads = [
        pltpu.make_async_copy(observed_ref, seen_ref, load_sem.at[0]),
        pltpu.make_async_copy(data_weight_ref, scale_ref, load_sem.at[1]),
    ]
    for load in loads:
        load.start()

    barrier = pltpu.get_barrier_semaphore()

    @pl.loop(1, owners)
    def _(step):
        pl.semaphore_signal(
            barrier, inc=1, device_id={"bin": partner(step)}, device_id_type=pl.DeviceIdType.MESH
        )

    def iota(shape, axis):
        return lax.broadcasted_iota(jnp.int32, shape, axis)

    wide = jnp.broadcast_to(bins_ref[...], (traces, traces)).astype(f32)
    tall = wide.T
    same = wide == tall
    above = iota((traces, traces), 0)
    beside = iota((traces, traces), 1)
    slot_row = wide[0:1, :] * per_bin + jnp.sum(
        jnp.where(same & (above < beside), 1.0, 0.0), axis=0, keepdims=True
    )
    slot_col = tall[:, 0:1] * per_bin + jnp.sum(
        jnp.where(same & (beside < above), 1.0, 0.0), axis=1, keepdims=True
    )
    pick = jnp.where(iota((slots, 1), 0).astype(f32) == slot_row, 1.0, 0.0).astype(bf16)
    pick_back = jnp.where(slot_col == iota((1, slots), 1).astype(f32), 1.0, 0.0).astype(bf16)
    mark = jnp.broadcast_to(offs_ref[...] + 1, (traces, traces)).astype(f32).T.astype(bf16)
    mark_out_ref[...] = jnp.dot(pick, mark, preferred_element_type=f32).astype(bf16)

    all_marks = (mark_out_ref, mark_in_ref, group, pl.ds(0, traces), mark_send, mark_recv)

    def forward(index):
        low = 0 if index == 0 else pieces[index][0] + 128
        high = samples if index == len(pieces) - 1 else pieces[index][1] + 128
        return low, high

    def forward_copy(index):
        low, high = forward(index)
        return (
            outgoing_ref,
            arrived_ref,
            group,
            pl.ds(low, high - low),
            out_send.at[index],
            out_recv.at[index],
        )

    def back_copy(index):
        low, high = pieces[index]
        return (
            answer_ref,
            returned_ref,
            group,
            pl.ds(low, high - low),
            back_send.at[index],
            back_recv.at[index],
        )

    def fill(index):
        low, high = forward(index)
        for lane in range(low, high, 128):
            outgoing_ref[:, pl.ds(lane, 128)] = jnp.dot(
                pick, pred_ref[:, pl.ds(lane, 128)], preferred_element_type=f32
            ).astype(bf16)

    mine = rows_of(me, group)
    fill(0)
    pl.semaphore_wait(barrier, owners - 1)
    start(*all_marks)
    start(*forward_copy(0))
    for index in range(1, len(pieces)):
        fill(index)
    mark_in_ref[mine, :] = mark_out_ref[mine, :]
    arrived_ref[mine, :] = outgoing_ref[mine, :]
    weights_body(conv_in_ref, conv_mid_ref, conv_out_ref, w_in_ref, w_mid_ref, w_out_ref)
    cells = 2 * OFFS
    nothing = jnp.zeros((8, cells), f32)
    natural_ref[pl.ds(0, 8), :] = nothing
    natural_ref[pl.ds(samples + 8, 8), :] = nothing

    wait_recv(*all_marks)
    cell = iota((slots, cells), 1)
    row = iota((slots, cells), 0)
    offset = (cell & (OFFS - 1)) + 1
    bin_of_row = lax.rem(row, group) >= per_bin
    bin_of_cell = cell >= OFFS
    hit = (mark_in_ref[...].astype(f32) == offset.astype(f32)) & (bin_of_row == bin_of_cell)
    cell_pick_wide = jnp.where(hit, 1.0, 0.0)
    cell_pick = cell_pick_wide.astype(bf16)
    cell_pick_back = cell_pick_wide.T.astype(bf16)

    blk = SEGS
    seg_index = iota((blk, 1), 0)

    def mask_rows(ref, first_row, edge):
        rows = pl.ds(first_row, blk)
        ref[rows, :] = jnp.where(seg_index == edge, 0.0, ref[rows, :].astype(f32)).astype(
            ref.dtype
        )

    total = jnp.zeros((8, 128), f32)
    for index, piece in enumerate(pieces):
        span = span_of(piece)
        at_start = index == 0
        at_end = index == len(pieces) - 1
        n_first = (span + 10) * blk
        n_second = (span + 2) * blk
        n_out = span * blk
        chunk_a = largest_chunk(span + 10, MOST) * blk
        chunk_b = largest_chunk(span + 2, MOST) * blk
        wait_recv(*forward_copy(index))
        if not at_end:
            start(*forward_copy(index + 1))
        for lane in range(*forward(index), 128):
            natural_ref[pl.ds(8 + lane, 128), :] = jnp.dot(
                cell_pick_back, arrived_ref[:, pl.ds(lane, 128)], preferred_element_type=f32
            ).T
        for seg in range(SEGS):
            ext_ref[pl.ds(seg, span + 12, stride=blk), :] = natural_ref[
                pl.ds(piece[0] + seg * span + 2, span + 12), :
            ]
        for which in range(2):
            for tap in range(3):
                p3_ref[which, pl.ds(0, n_first), pl.ds(tap * OFFS, OFFS)] = ext_ref[
                    pl.ds(tap * blk, n_first), :
                ][:, which * OFFS : (which + 1) * OFFS].astype(bf16)

        @pl.loop(0, 2)
        def _(which):
            @pl.loop(0, n_first // chunk_a)
            def _(step):
                rows = pl.ds(pl.multiple_of(step * chunk_a, 16), chunk_a)
                window = p3_ref[which, rows, :]
                for tile in range(TILES):
                    lanes = pl.ds(tile * TILE, TILE)
                    half = jnp.dot(window, w_in_ref[:, lanes], preferred_element_type=f32)
                    h1_ref[rows, lanes] = (half + half * jnp.tanh(half)).astype(bf16)

            for b in range(5):
                if at_start:
                    mask_rows(h1_ref, b * blk, 0)
                if at_end:
                    mask_rows(h1_ref, (span + 5 + b) * blk, SEGS - 1)

            @pl.loop(0, n_second // chunk_b)
            def _(step):
                base = pl.multiple_of(step * chunk_b, 16)
                acc = jnp.zeros((chunk_b, 3 * OFFS), f32)
                for tile in range(TILES):
                    rows, first = middle_rows(h1_ref, base, chunk_b, tile)
                    half = jnp.dot(
                        rows,
                        w_mid_ref[1 if tile == SPLIT_TILE else 0],
                        preferred_element_type=f32,
                    )
                    second = first.astype(f32) + (half + half * jnp.tanh(half))
                    acc = acc + jnp.dot(
                        second.astype(bf16),
                        w_out_ref[pl.ds(tile * TILE, TILE), :],
                        preferred_element_type=f32,
                    )
                z_ref[which, pl.ds(base, chunk_b), :] = acc

        for which in range(2):
            if at_start:
                mask_rows(z_ref.at[which], 0, 0)
            if at_end:
                mask_rows(z_ref.at[which], (span + 1) * blk, SEGS - 1)

        @pl.loop(0, 8)
        def _(step):
            size = n_out // 8
            base = pl.multiple_of(step * size, 16)
            sums = []
            for which in range(2):
                left = z_ref[which, pl.ds(base, size), :][:, 0:OFFS]
                mid = z_ref[which, pl.ds(base + blk, size), :][:, OFFS : 2 * OFFS]
                right = z_ref[which, pl.ds(base + 2 * blk, size), :][:, 2 * OFFS : 3 * OFFS]
                sums.append(left + mid + right)
            centre = ext_ref[pl.ds(base + 6 * blk, size), :]
            ext_ref[pl.ds(base, size), :] = centre + jnp.concatenate(sums, axis=1)

        for seg in range(SEGS):
            back_ref[pl.ds(seg * span, span), :] = ext_ref[pl.ds(seg, span, stride=blk), :]
        for lane in range(0, n_out, 128):
            answer_ref[:, pl.ds(piece[0] + lane, 128)] = jnp.dot(
                cell_pick,
                back_ref[pl.ds(lane, 128), :].T.astype(bf16),
                preferred_element_type=f32,
            ).astype(bf16)
        start(*back_copy(index))

    returned_ref[mine, :] = answer_ref[mine, :]
    for load in loads:
        load.wait()
    for index, piece in enumerate(pieces):
        wait_recv(*back_copy(index))
        for lane in range(*piece, 128):
            lanes = pl.ds(lane, 128)
            own = jnp.dot(pick_back, returned_ref[:, lanes], preferred_element_type=f32)
            miss = scale_ref[:, lanes] * (own - seen_ref[:, lanes])
            misfit_ref[:, lanes] = miss
            total = total + jnp.sum((miss * miss).reshape(traces // 8, 8, 128), axis=0)

    part_ref[...] = total

    def part_copy(step, here):
        other = partner(step)
        return pltpu.make_async_remote_copy(
            src_ref=part_ref,
            dst_ref=parts_ref.at[rows_of(me if here else other, 8), :],
            send_sem=part_send.at[other],
            recv_sem=part_recv.at[me if here else other],
            device_id={"bin": other},
            device_id_type=pl.DeviceIdType.MESH,
        )

    @pl.loop(1, owners)
    def _(step):
        part_copy(step, True).start()

    parts_ref[rows_of(me, 8), :] = total

    @pl.loop(1, owners)
    def _(step):
        part_copy(step, False).wait_recv()

    mean_square = jnp.sum(parts_ref[...], keepdims=True) / (traces * owners * samples)
    factor_ref[...] = jnp.broadcast_to(lax.rsqrt(mean_square + 1e-05), factor_ref.shape)

    @pl.loop(1, owners)
    def _(step):
        part_copy(step, True).wait_send()

    wait_send(*all_marks)
    for index in range(len(pieces)):
        wait_send(*forward_copy(index))
        wait_send(*back_copy(index))


def fused(predicted, observed, data_weight, bin_ids, offset_slots, conv_in, conv_mid, conv_out):
    traces, samples = predicted.shape
    owners = lax.axis_size("bin")
    group = traces // OFFS * (traces // owners)
    slots = owners * group
    pieces = gathered_pieces(samples)
    count = len(pieces)
    span = max(span_of(piece) for piece in pieces)
    cells = 2 * OFFS
    bf16 = jnp.bfloat16
    f32 = jnp.float32
    dma = pltpu.SemaphoreType.DMA
    vmem = pl.BlockSpec(memory_space=pltpu.VMEM)
    anywhere = pl.BlockSpec(memory_space=pl.ANY)

    def body(*refs):
        fused_body(owners, *refs)

    misfit, factor = pl.pallas_call(
        body,
        out_shape=(
            jax.ShapeDtypeStruct((traces, samples), f32),
            jax.ShapeDtypeStruct((8, 128), f32),
        ),
        in_specs=[vmem, vmem, vmem, anywhere, anywhere, vmem, vmem, vmem],
        out_specs=[vmem, vmem],
        scratch_shapes=[
            pltpu.VMEM((3 * OFFS, TILES * TILE), bf16),
            pltpu.VMEM((2, 4 * TILE, TILE), bf16),
            pltpu.VMEM((TILES * TILE, 3 * OFFS), bf16),
            pltpu.VMEM((slots, traces), bf16),
            pltpu.VMEM((slots, traces), bf16),
            pltpu.VMEM((slots, samples), bf16),
            pltpu.VMEM((slots, samples), bf16),
            pltpu.VMEM((slots, samples), bf16),
            pltpu.VMEM((slots, samples), bf16),
            pltpu.VMEM((traces, samples), f32),
            pltpu.VMEM((traces, samples), f32),
            pltpu.VMEM((samples + 16, cells), f32),
            pltpu.VMEM(((span + 12) * SEGS, cells), f32),
            pltpu.VMEM((2, (span + 10) * SEGS, 3 * OFFS), bf16),
            pltpu.VMEM(((span + 10) * SEGS, TILES * TILE), bf16),
            pltpu.VMEM((2, (span + 2) * SEGS, 3 * OFFS), f32),
            pltpu.VMEM((span * SEGS, cells), f32),
            pltpu.VMEM((8, 128), f32),
            pltpu.VMEM((8 * owners, 128), f32),
            dma((2,)),
            dma((owners,)),
            dma((owners,)),
            dma((count, owners)),
            dma((count, owners)),
            dma((count, owners)),
            dma((count, owners)),
            dma((owners,)),
            dma((owners,)),
        ],
        compiler_params=pltpu.CompilerParams(
            collective_id=0, has_side_effects=True, vmem_limit_bytes=56 * 1024 * 1024
        ),
        name="exchange_filter",
    )(
        predicted,
        bin_ids.reshape(1, traces),
        offset_slots.reshape(1, traces),
        observed,
        data_weight,
        conv_in,
        conv_mid.reshape(9 * CHAN, CHAN),
        conv_out,
    )
    return (misfit * factor[0, 0]).astype(bf16)


def local(*args):
    traces = args[0].shape[0]
    owners = lax.axis_size("bin")
    if traces // OFFS * (traces // owners) % 16 == 0:
        return fused(*args)
    return by_ops(*args)


def solution(mesh):
    in_specs = (
        P(("line", "bin"), None),
        P(("line", "bin"), None),
        P(("line", "bin"), None),
        P(("line", "bin")),
        P(("line", "bin")),
        P(),
        P(),
        P(),
    )
    out_specs = P(("line", "bin"), None)
    return jax.shard_map(local, mesh=mesh, in_specs=in_specs, out_specs=out_specs, check_vma=False)
```

```python
import jax
import jax.numpy as jnp
from jax import lax
from jax.experimental import pallas as pl
from jax.experimental.pallas import tpu as pltpu
from jax.sharding import PartitionSpec as P

OFFS = 64
CHAN = 48
SEGS = 16
MOST = 46
TILE = 256
CUTS = (4, 13)
BLK = 8
CELLS = TILE // CHAN
SPARE = TILE - CELLS * CHAN
TILES = -(-OFFS // CELLS)
SPLIT_TILE = OFFS // 2 // CELLS
SPLIT = OFFS // 2 % CELLS


def kernel_body(
    span,
    chunk_a,
    chunk_b,
    panel_ref,
    w_in_ref,
    w_mid_ref,
    w_out_ref,
    out_ref,
    ext_ref,
    p3_ref,
    h1_ref,
    z_ref,
):
    blk = SEGS
    n_first = (span + 10) * blk
    n_second = (span + 2) * blk
    for seg in range(SEGS):
        ext_ref[pl.ds(6 * blk + seg, span, stride=blk), :] = panel_ref[
            pl.ds(seg * span, span), :
        ].astype(jnp.float32)
    edge = jnp.zeros((1, OFFS), jnp.float32)
    for b in range(6):
        ext_ref[pl.ds(b * blk, 1), :] = edge
        ext_ref[pl.ds(b * blk + 1, blk - 1), :] = ext_ref[pl.ds((b + span) * blk, blk - 1), :]
        last = (span + 6 + b) * blk
        ext_ref[pl.ds(last, blk - 1), :] = ext_ref[pl.ds((6 + b) * blk + 1, blk - 1), :]
        ext_ref[pl.ds(last + blk - 1, 1), :] = edge
    for tap in range(3):
        p3_ref[:, pl.ds(tap * OFFS, OFFS)] = ext_ref[pl.ds(tap * blk, n_first), :].astype(
            jnp.bfloat16
        )
    @pl.loop(0, n_first // chunk_a)
    def _(step):
        rows = pl.ds(pl.multiple_of(step * chunk_a, 16), chunk_a)
        window = p3_ref[rows, :]
        for tile in range(TILES):
            lanes = pl.ds(tile * TILE, TILE)
            half = jnp.dot(window, w_in_ref[:, lanes], preferred_element_type=jnp.float32)
            h1_ref[rows, lanes] = (half + half * jnp.tanh(half)).astype(jnp.bfloat16)

    seg = lax.broadcasted_iota(jnp.int32, (blk, 1), 0)
    for b in range(5):
        head = pl.ds(b * blk, blk)
        h1_ref[head, :] = jnp.where(seg == 0, 0.0, h1_ref[head, :].astype(jnp.float32)).astype(
            jnp.bfloat16
        )
        tail = pl.ds((span + 5 + b) * blk, blk)
        h1_ref[tail, :] = jnp.where(
            seg == SEGS - 1, 0.0, h1_ref[tail, :].astype(jnp.float32)
        ).astype(jnp.bfloat16)

    @pl.loop(0, n_second // chunk_b)
    def _(step):
        base = pl.multiple_of(step * chunk_b, 16)
        total = jnp.zeros((chunk_b, 3 * OFFS), jnp.float32)
        for tile in range(TILES):
            rows, first = middle_rows(h1_ref, base, chunk_b, tile, blk)
            half = jnp.dot(
                rows,
                w_mid_ref[1 if tile == SPLIT_TILE else 0],
                preferred_element_type=jnp.float32,
            )
            second = first.astype(jnp.float32) + (half + half * jnp.tanh(half))
            total = total + jnp.dot(
                second.astype(jnp.bfloat16),
                w_out_ref[pl.ds(tile * TILE, TILE), :],
                preferred_element_type=jnp.float32,
            )
        z_ref[pl.ds(base, chunk_b), :] = total

    z_ref[pl.ds(0, blk), :] = jnp.where(seg == 0, 0.0, z_ref[pl.ds(0, blk), :])
    last = pl.ds((span + 1) * blk, blk)
    z_ref[last, :] = jnp.where(seg == SEGS - 1, 0.0, z_ref[last, :])

    n_out = span * blk

    @pl.loop(0, 8)
    def _(step):
        size = n_out // 8
        base = pl.multiple_of(step * size, 16)
        left = z_ref[pl.ds(base, size), :][:, 0:OFFS]
        mid = z_ref[pl.ds(base + blk, size), :][:, OFFS : 2 * OFFS]
        right = z_ref[pl.ds(base + 2 * blk, size), :][:, 2 * OFFS : 3 * OFFS]
        centre = p3_ref[pl.ds(base + 5 * blk, size), :].astype(jnp.float32)[:, OFFS : 2 * OFFS]
        ext_ref[pl.ds(base, size), :] = centre + (left + mid + right)

    for seg in range(SEGS):
        out_ref[pl.ds(seg * span, span), :] = ext_ref[
            pl.ds(seg, span, stride=blk), :
        ].astype(jnp.bfloat16)


def largest_chunk(blocks, most):
    return max(d for d in range(1, most + 1) if blocks % d == 0)


def by_chan(v):
    return (v * 43691) >> 21


def one_hot(hit, value):
    return jnp.where(hit, value, 0.0).astype(jnp.bfloat16)


def column(conv_out_ref, a, d):
    row = lax.broadcasted_iota(jnp.int32, (CHAN, CHAN), 0)
    lane = lax.broadcasted_iota(jnp.int32, (CHAN, CHAN), 1)
    taps = jnp.where(row == lane, conv_out_ref[a, d : d + 1, :].astype(jnp.float32), 0.0)
    return jnp.sum(taps, axis=1, keepdims=True)


def weights_body(conv_in_ref, conv_mid_ref, conv_out_ref, w_in_ref, w_mid_ref, w_out_ref):
    f32 = jnp.float32

    def iota(shape, axis):
        return lax.broadcasted_iota(jnp.int32, shape, axis)

    def offset_of(place):
        return jnp.where(place < OFFS // 2, 2 * place, 2 * place - OFFS + 1)

    def cell_of(lane):
        cell = by_chan(lane)
        spare = cell >= CELLS
        return jnp.where(spare, -1, cell), jnp.where(spare, lane - CELLS * CHAN, lane - CHAN * cell)

    others = iota((OFFS, 1), 0) + 1
    chan_down = iota((CHAN, 1), 0)
    chan_across = iota((1, CHAN), 1)

    slot_in, chan_in = cell_of(iota((1, TILE), 1))
    spread = one_hot(chan_in == chan_down, 0.5)
    wide_in = [jnp.dot(conv_in_ref[a], spread, preferred_element_type=f32) for a in range(3)]

    @pl.loop(0, TILES)
    def _(tile):
        base = pl.multiple_of(tile * TILE, TILE)
        near = others - offset_of(slot_in + CELLS * tile)
        for d in range(3):
            value = jnp.zeros((OFFS, TILE), f32)
            for a in range(3):
                value = jnp.where(near == a, wide_in[a][d : d + 1, :], value)
            w_in_ref[pl.ds(d * OFFS, OFFS), pl.ds(base, TILE)] = value.astype(jnp.bfloat16)

    y = iota((1, TILE), 1)
    slot_y = by_chan(y)
    spread_y = one_hot((y - CHAN * slot_y == chan_down) & (slot_y < CELLS), 0.5)
    wide = jnp.dot(conv_mid_ref[...], spread_y, preferred_element_type=f32)

    def taps_of(a, d):
        start = (a * 3 + d) * CHAN
        return wide[start : start + CHAN, :]

    x = iota((TILE, 1), 0)
    slot_x, chan_x = cell_of(x)
    pick = one_hot(chan_x == chan_across, 1.0)
    step = slot_x - slot_y + 1
    apart = (slot_x < SPLIT) != (slot_y < SPLIT)
    for d in range(3):
        value = jnp.zeros((TILE, TILE), f32)
        for a in range(3):
            part = jnp.dot(pick, taps_of(a, d).astype(jnp.bfloat16), preferred_element_type=f32)
            value = jnp.where(step == a, part, value)
        w_mid_ref[0, pl.ds(d * TILE, TILE), :] = value.astype(jnp.bfloat16)
        w_mid_ref[1, pl.ds(d * TILE, TILE), :] = jnp.where(
            apart & (slot_x >= 0), 0.0, value
        ).astype(jnp.bfloat16)
    edge = jnp.zeros((TILE, TILE), f32)
    for d, right, left in ((0, 0, 80), (1, 128, 48), (2, 176, 224)):
        from_right = one_hot((x - right == chan_across) & (x < right + CHAN), 1.0)
        from_left = one_hot(
            (x - left + SPARE == chan_across) & (x >= left) & (x < left + CHAN - SPARE), 1.0
        )
        low = jnp.where(slot_y == 0, taps_of(0, d), 0.0).astype(jnp.bfloat16)
        high = jnp.where(slot_y == CELLS - 1, taps_of(2, d), 0.0).astype(jnp.bfloat16)
        edge = edge + jnp.dot(from_right, high, preferred_element_type=f32)
        edge = edge + jnp.dot(from_left, low, preferred_element_type=f32)
    for kind in range(2):
        w_mid_ref[kind, pl.ds(3 * TILE, TILE), :] = edge.astype(jnp.bfloat16)

    triple = iota((1, 3 * OFFS), 1)
    group = triple // OFFS
    wide_out = []
    for a in range(3):
        value = jnp.zeros((CHAN, 3 * OFFS), f32)
        for d in range(3):
            value = jnp.where(group == d, column(conv_out_ref, a, d), value)
        wide_out.append(value.astype(jnp.bfloat16))
    across = one_hot((chan_x == chan_across) & (slot_x >= 0), 1.0)
    parts = [jnp.dot(across, wide_out[a], preferred_element_type=f32) for a in range(3)]

    @pl.loop(0, TILES)
    def _(tile):
        base = pl.multiple_of(tile * TILE, TILE)
        near = offset_of(slot_x + CELLS * tile) + 1 - (triple - OFFS * group)
        value = jnp.zeros((TILE, 3 * OFFS), f32)
        for a in range(3):
            value = jnp.where(near == a, parts[a], value)
        w_out_ref[pl.ds(base, TILE), :] = value.astype(jnp.bfloat16)


def middle_rows(h1_ref, base, chunk, tile, blk):
    lane = lax.broadcasted_iota(jnp.int32, (1, 128), 1)

    def piece(start, width, tap):
        return h1_ref[pl.ds(base + 4 * blk * tap, chunk), pl.ds(start, width)]

    after = min(tile + 1, TILES - 1) * TILE
    right = [piece(after, 128, tap) for tap in range(3)]
    if tile == 0:
        left = [jnp.zeros((chunk, 128), jnp.bfloat16)] * 3
        turned = left
    else:
        left = [piece(tile * TILE - 128, 128, tap) for tap in range(3)]
        turned = [None, pltpu.roll(left[1], 96, 1), pltpu.roll(left[2], 16, 1)]
    low = jnp.where(lane < 48, right[0], jnp.where(lane < 80, turned[1], left[0]))
    high = jnp.where(
        lane < 48, right[1], jnp.where(lane < 96, pltpu.roll(right[2], 48, 1), turned[2])
    )
    whole = [piece(tile * TILE, TILE, tap) for tap in range(3)]
    return jnp.concatenate(whole + [low, high], axis=1), whole[1]


def band_weights(conv_in, conv_mid, conv_out):
    bf16 = jnp.bfloat16
    return pl.pallas_call(
        weights_body,
        out_shape=(
            jax.ShapeDtypeStruct((3 * OFFS, TILES * TILE), bf16),
            jax.ShapeDtypeStruct((2, 4 * TILE, TILE), bf16),
            jax.ShapeDtypeStruct((TILES * TILE, 3 * OFFS), bf16),
        ),
        in_specs=[pl.BlockSpec(memory_space=pltpu.VMEM)] * 3,
        out_specs=[pl.BlockSpec(memory_space=pltpu.VMEM)] * 3,
        compiler_params=pltpu.CompilerParams(vmem_limit_bytes=40 * 1024 * 1024),
        name="band_weights",
    )(conv_in, conv_mid.reshape(9 * CHAN, CHAN), conv_out)


def filter_rows(panel, weights):
    samples, offs = panel.shape
    span = samples // SEGS
    blk = SEGS
    chunk_a = largest_chunk(span + 10, MOST) * blk
    chunk_b = largest_chunk(span + 2, MOST) * blk

    def body(*refs):
        kernel_body(span, chunk_a, chunk_b, *refs)

    return pl.pallas_call(
        body,
        out_shape=jax.ShapeDtypeStruct((span * blk, offs), jnp.bfloat16),
        in_specs=[pl.BlockSpec(memory_space=pltpu.VMEM)] * 4,
        out_specs=pl.BlockSpec(memory_space=pltpu.VMEM),
        scratch_shapes=[
            pltpu.VMEM(((span + 12) * blk, offs), jnp.float32),
            pltpu.VMEM(((span + 10) * blk, 3 * offs), jnp.bfloat16),
            pltpu.VMEM(((span + 10) * blk, TILES * TILE), jnp.bfloat16),
            pltpu.VMEM(((span + 2) * blk, 3 * offs), jnp.float32),
        ],
        compiler_params=pltpu.CompilerParams(vmem_limit_bytes=48 * 1024 * 1024),
        name="panel_filter",
    )(panel, *weights)


def by_ops(predicted, observed, data_weight, bin_ids, offset_slots, conv_in, conv_mid, conv_out):
    tr_dev, samples = predicted.shape
    owners = lax.axis_size("bin")
    bin_dev = tr_dev // OFFS
    capacity = max(1, tr_dev // owners)
    slots = owners * capacity
    row_index = jnp.arange(tr_dev, dtype=jnp.int32)
    earlier = row_index[None, :] < row_index[:, None]
    same_bin = bin_ids[:, None] == bin_ids[None, :]
    position = jnp.sum((same_bin & earlier).astype(jnp.int32), axis=1)
    owner_slot = (bin_ids // bin_dev) * capacity + position
    local_bin = bin_ids % bin_dev
    mark = jnp.broadcast_to((offset_slots + 1).astype(jnp.bfloat16)[:, None], (tr_dev, 128))
    labelled = jnp.concatenate([predicted, mark], axis=1)
    slot_index = jnp.arange(slots, dtype=jnp.int32)
    offsets = jnp.arange(OFFS, dtype=jnp.int32)

    picks = []
    arrivals = []
    for b in range(bin_dev):
        send_slot = jnp.where(local_bin == b, owner_slot, -1)
        pick = (slot_index[:, None] == send_slot[None, :]).astype(jnp.bfloat16)
        outgoing = jnp.dot(pick, labelled, preferred_element_type=jnp.float32)
        outgoing = outgoing.astype(jnp.bfloat16).reshape(owners, capacity, samples + 128)
        if b == 0:
            outgoing, conv_in, conv_mid, conv_out = lax.optimization_barrier(
                (outgoing, conv_in, conv_mid, conv_out)
            )
            weights = band_weights(conv_in, conv_mid, conv_out)
        else:
            outgoing, weights = lax.optimization_barrier((outgoing, weights))
        arrived = lax.all_to_all(outgoing, "bin", split_axis=0, concat_axis=0, tiled=True)
        picks.append(pick)
        arrivals.append(arrived.reshape(slots, samples + 128))

    own_rows = 0.0
    for b in range(bin_dev):
        cell = arrivals[b][:, samples].astype(jnp.int32) - 1
        cell_pick = (cell[:, None] == offsets[None, :]).astype(jnp.bfloat16)
        panel = jnp.einsum(
            "sc,st->tc",
            cell_pick,
            arrivals[b][:, :samples],
            preferred_element_type=jnp.float32,
        ).astype(jnp.bfloat16)
        filtered = filter_rows(panel, weights)
        answer = jnp.einsum("sc,tc->st", cell_pick, filtered, preferred_element_type=jnp.float32)
        answer = answer.astype(jnp.bfloat16).reshape(owners, capacity, samples)
        returned = lax.all_to_all(answer, "bin", split_axis=0, concat_axis=0, tiled=True)
        own_rows = own_rows + jnp.einsum(
            "sr,st->rt",
            picks[b],
            returned.reshape(slots, samples),
            preferred_element_type=jnp.float32,
        )
    misfit = data_weight * (own_rows - observed)
    share = jnp.broadcast_to(jnp.sum(misfit * misfit), (owners, 1, 128))
    shares = lax.all_to_all(share, "bin", split_axis=0, concat_axis=0, tiled=True)
    misfit_total = jnp.sum(shares[:, 0, 0])
    mean_square = misfit_total / (tr_dev * owners * samples)
    return (misfit * lax.rsqrt(mean_square + 1e-05)).astype(jnp.bfloat16)


def steps_for(rows):
    units = rows // 16
    steps = -(-units // MOST)
    return steps, -(-units // steps) * 16


def gathered_pieces(samples):
    cuts = [0] + [samples * part // 16 for part in CUTS] + [samples]
    return list(zip(cuts[:-1], cuts[1:]))


def span_of(piece):
    return (piece[1] - piece[0]) // BLK


def fused_body(
    owners,
    pred_ref,
    bins_ref,
    offs_ref,
    observed_ref,
    data_weight_ref,
    conv_in_ref,
    conv_mid_ref,
    conv_out_ref,
    out_ref,
    w_in_ref,
    w_mid_ref,
    w_out_ref,
    mark_out_ref,
    mark_in_ref,
    outgoing_ref,
    arrived_ref,
    answer_ref,
    returned_ref,
    seen_ref,
    scale_ref,
    misfit_ref,
    natural_ref,
    ext_ref,
    p3_ref,
    h1_ref,
    z_ref,
    back_ref,
    part_ref,
    parts_ref,
    load_sem,
    mark_send,
    mark_recv,
    out_send,
    out_recv,
    back_send,
    back_recv,
    part_send,
    part_recv,
):
    f32 = jnp.float32
    bf16 = jnp.bfloat16
    traces, samples = pred_ref.shape
    group = traces // OFFS * (traces // owners)
    slots = owners * group
    per_bin = traces // owners
    pieces = gathered_pieces(samples)
    me = lax.axis_index("bin")

    def partner(step):
        return lax.rem(me + step, owners)

    def rows_of(index, size):
        return pl.ds(pl.multiple_of(index * size, size), size)

    def copy_to(step, source, target, size, lanes, sent, got):
        to = partner(step)
        return pltpu.make_async_remote_copy(
            src_ref=source.at[rows_of(to, size), lanes],
            dst_ref=target.at[rows_of(me, size), lanes],
            send_sem=sent,
            recv_sem=got,
            device_id={"bin": to},
            device_id_type=pl.DeviceIdType.MESH,
        )

    def all_of(source, target, size, lanes, sent, got):
        rows = pl.ds(0, (owners - 1) * size)
        return pltpu.make_async_remote_copy(
            src_ref=source.at[rows, lanes],
            dst_ref=target.at[rows, lanes],
            send_sem=sent,
            recv_sem=got,
            device_id={"bin": partner(1)},
            device_id_type=pl.DeviceIdType.MESH,
        )

    def start(*what):
        @pl.loop(1, owners)
        def _(step):
            copy_to(step, *what).start()

    def wait_recv(*what):
        all_of(*what).wait_recv()

    def wait_send(*what):
        all_of(*what).wait_send()

    loads = [
        pltpu.make_async_copy(observed_ref, seen_ref, load_sem.at[0]),
        pltpu.make_async_copy(data_weight_ref, scale_ref, load_sem.at[1]),
    ]
    for load in loads:
        load.start()

    barrier = pltpu.get_barrier_semaphore()

    @pl.loop(1, owners)
    def _(step):
        pl.semaphore_signal(
            barrier, inc=1, device_id={"bin": partner(step)}, device_id_type=pl.DeviceIdType.MESH
        )

    def iota(shape, axis):
        return lax.broadcasted_iota(jnp.int32, shape, axis)

    wide = jnp.broadcast_to(bins_ref[...], (traces, traces)).astype(f32)
    tall = wide.T
    same = wide == tall
    above = iota((traces, traces), 0)
    beside = iota((traces, traces), 1)
    slot_row = wide[0:1, :] * per_bin + jnp.sum(
        jnp.where(same & (above < beside), 1.0, 0.0), axis=0, keepdims=True
    )
    slot_col = tall[:, 0:1] * per_bin + jnp.sum(
        jnp.where(same & (beside < above), 1.0, 0.0), axis=1, keepdims=True
    )
    pick = jnp.where(iota((slots, 1), 0).astype(f32) == slot_row, 1.0, 0.0).astype(bf16)
    pick_back = jnp.where(slot_col == iota((1, slots), 1).astype(f32), 1.0, 0.0).astype(bf16)
    mark = jnp.broadcast_to(offs_ref[...] + 1, (traces, traces)).astype(f32).T.astype(bf16)
    mark_out_ref[...] = jnp.dot(pick, mark, preferred_element_type=f32).astype(bf16)

    all_marks = (mark_out_ref, mark_in_ref, group, pl.ds(0, traces), mark_send, mark_recv)

    def forward(index):
        low = 0 if index == 0 else pieces[index][0] + 128
        high = samples if index == len(pieces) - 1 else pieces[index][1] + 128
        return low, high

    def forward_copy(index):
        low, high = forward(index)
        return (
            outgoing_ref,
            arrived_ref,
            group,
            pl.ds(low, high - low),
            out_send.at[index],
            out_recv.at[index],
        )

    def back_copy(index):
        low, high = pieces[index]
        return (
            answer_ref,
            returned_ref,
            group,
            pl.ds(low, high - low),
            back_send.at[index],
            back_recv.at[index],
        )

    def fill(index):
        low, high = forward(index)
        for lane in range(low, high, 128):
            outgoing_ref[:, pl.ds(lane, 128)] = jnp.dot(
                pick, pred_ref[:, pl.ds(lane, 128)], preferred_element_type=f32
            ).astype(bf16)

    mine = rows_of(me, group)
    fill(0)
    pl.semaphore_wait(barrier, owners - 1)
    start(*all_marks)
    start(*forward_copy(0))
    for index in range(1, len(pieces)):
        fill(index)
    mark_in_ref[mine, :] = mark_out_ref[mine, :]
    arrived_ref[mine, :] = outgoing_ref[mine, :]
    weights_body(conv_in_ref, conv_mid_ref, conv_out_ref, w_in_ref, w_mid_ref, w_out_ref)
    cells = 2 * OFFS
    nothing = jnp.zeros((8, cells), f32)
    natural_ref[pl.ds(0, 8), :] = nothing
    natural_ref[pl.ds(samples + 8, 8), :] = nothing

    wait_recv(*all_marks)
    cell = iota((slots, cells), 1)
    row = iota((slots, cells), 0)
    offset = (cell & (OFFS - 1)) + 1
    bin_of_row = lax.rem(row, group) >= per_bin
    bin_of_cell = cell >= OFFS
    hit = (mark_in_ref[...].astype(f32) == offset.astype(f32)) & (bin_of_row == bin_of_cell)
    cell_pick_wide = jnp.where(hit, 1.0, 0.0)
    cell_pick = cell_pick_wide.astype(bf16)
    cell_pick_back = cell_pick_wide.T.astype(bf16)

    blk = BLK

    def mask_rows(ref, first_row, count, outside):
        rows = pl.ds(first_row, count)
        row = iota((count, 1), 0)
        ref[rows, :] = jnp.where(outside(row), 0.0, ref[rows, :].astype(f32)).astype(ref.dtype)

    def before(row):
        return ((row & (blk - 1)) == 0) & (row < 5 * blk)

    def behind(row):
        return ((row & (blk - 1)) == blk - 1) & (row >= blk)

    total = jnp.zeros((8, 128), f32)
    for index, piece in enumerate(pieces):
        span = span_of(piece)
        at_start = index == 0
        at_end = index == len(pieces) - 1
        n_first = (span + 10) * blk
        n_second = (span + 2) * blk
        n_out = span * blk
        steps_a, chunk_a = steps_for(n_first)
        steps_b, chunk_b = steps_for(n_second)
        wait_recv(*forward_copy(index))
        if not at_end:
            start(*forward_copy(index + 1))
        for lane in range(*forward(index), 128):
            natural_ref[pl.ds(8 + lane, 128), :] = jnp.dot(
                cell_pick_back, arrived_ref[:, pl.ds(lane, 128)], preferred_element_type=f32
            ).T
        for seg in range(BLK):
            ext_ref[pl.ds(seg, span + 12, stride=blk), :] = natural_ref[
                pl.ds(piece[0] + seg * span + 2, span + 12), :
            ]
        for which in range(2):
            for tap in range(3):
                p3_ref[which, pl.ds(0, n_first), pl.ds(tap * OFFS, OFFS)] = ext_ref[
                    pl.ds(tap * blk, n_first), :
                ][:, which * OFFS : (which + 1) * OFFS].astype(bf16)

        @pl.loop(0, 2)
        def _(which):
            @pl.loop(0, steps_a)
            def _(step):
                rows = pl.ds(pl.multiple_of(step * chunk_a, 16), chunk_a)
                window = p3_ref[which, rows, :]
                for tile in range(TILES):
                    lanes = pl.ds(tile * TILE, TILE)
                    half = jnp.dot(window, w_in_ref[:, lanes], preferred_element_type=f32)
                    h1_ref[rows, lanes] = (half + half * jnp.tanh(half)).astype(bf16)

            if at_start:
                mask_rows(h1_ref, 0, 6 * blk, before)
            if at_end:
                mask_rows(h1_ref, (span + 4) * blk, 6 * blk, behind)

            @pl.loop(0, steps_b)
            def _(step):
                base = pl.multiple_of(step * chunk_b, 16)
                acc = jnp.zeros((chunk_b, 3 * OFFS), f32)
                for tile in range(TILES):
                    rows, first = middle_rows(h1_ref, base, chunk_b, tile, blk)
                    half = jnp.dot(
                        rows,
                        w_mid_ref[1 if tile == SPLIT_TILE else 0],
                        preferred_element_type=f32,
                    )
                    second = first.astype(f32) + (half + half * jnp.tanh(half))
                    acc = acc + jnp.dot(
                        second.astype(bf16),
                        w_out_ref[pl.ds(tile * TILE, TILE), :],
                        preferred_element_type=f32,
                    )
                z_ref[which, pl.ds(base, chunk_b), :] = acc

        for which in range(2):
            if at_start:
                mask_rows(z_ref.at[which], 0, blk, lambda row: row == 0)
            if at_end:
                mask_rows(z_ref.at[which], (span + 1) * blk, blk, lambda row: row == blk - 1)

        @pl.loop(0, 8)
        def _(step):
            size = n_out // 8
            base = pl.multiple_of(step * size, 16)
            sums = []
            for which in range(2):
                left = z_ref[which, pl.ds(base, size), :][:, 0:OFFS]
                mid = z_ref[which, pl.ds(base + blk, size), :][:, OFFS : 2 * OFFS]
                right = z_ref[which, pl.ds(base + 2 * blk, size), :][:, 2 * OFFS : 3 * OFFS]
                sums.append(left + mid + right)
            centre = ext_ref[pl.ds(base + 6 * blk, size), :]
            ext_ref[pl.ds(base, size), :] = centre + jnp.concatenate(sums, axis=1)

        for seg in range(BLK):
            back_ref[pl.ds(seg * span, span), :] = ext_ref[pl.ds(seg, span, stride=blk), :]
        for lane in range(0, n_out, 128):
            answer_ref[:, pl.ds(piece[0] + lane, 128)] = jnp.dot(
                cell_pick,
                back_ref[pl.ds(lane, 128), :].T.astype(bf16),
                preferred_element_type=f32,
            ).astype(bf16)
        start(*back_copy(index))

    returned_ref[mine, :] = answer_ref[mine, :]
    for load in loads:
        load.wait()
    for index, piece in enumerate(pieces):
        wait_recv(*back_copy(index))
        for lane in range(*piece, 128):
            lanes = pl.ds(lane, 128)
            own = jnp.dot(pick_back, returned_ref[:, lanes], preferred_element_type=f32)
            miss = scale_ref[:, lanes] * (own - seen_ref[:, lanes])
            misfit_ref[:, lanes] = miss
            total = total + jnp.sum((miss * miss).reshape(traces // 8, 8, 128), axis=0)

    part_ref[...] = total

    @pl.loop(1, owners)
    def _(step):
        pltpu.make_async_remote_copy(
            src_ref=part_ref,
            dst_ref=parts_ref.at[rows_of(me, 8), :],
            send_sem=part_send,
            recv_sem=part_recv,
            device_id={"bin": partner(step)},
            device_id_type=pl.DeviceIdType.MESH,
        ).start()

    all_parts = (parts_ref, parts_ref, 8, pl.ds(0, 128), part_send, part_recv)
    parts_ref[rows_of(me, 8), :] = total
    wait_recv(*all_parts)
    mean_square = jnp.sum(parts_ref[...], keepdims=True) / (traces * owners * samples)
    out_ref[...] = (misfit_ref[...] * lax.rsqrt(mean_square + 1e-05)).astype(bf16)

    wait_send(*all_parts)
    wait_send(*all_marks)
    for index in range(len(pieces)):
        wait_send(*forward_copy(index))
        wait_send(*back_copy(index))


def fused(predicted, observed, data_weight, bin_ids, offset_slots, conv_in, conv_mid, conv_out):
    traces, samples = predicted.shape
    owners = lax.axis_size("bin")
    group = traces // OFFS * (traces // owners)
    slots = owners * group
    pieces = gathered_pieces(samples)
    count = len(pieces)
    span = max(span_of(piece) for piece in pieces)
    cells = 2 * OFFS
    bf16 = jnp.bfloat16
    f32 = jnp.float32
    dma = pltpu.SemaphoreType.DMA
    vmem = pl.BlockSpec(memory_space=pltpu.VMEM)
    anywhere = pl.BlockSpec(memory_space=pl.ANY)

    def body(*refs):
        fused_body(owners, *refs)

    return pl.pallas_call(
        body,
        out_shape=jax.ShapeDtypeStruct((traces, samples), bf16),
        in_specs=[vmem, vmem, vmem, anywhere, anywhere, vmem, vmem, vmem],
        out_specs=vmem,
        scratch_shapes=[
            pltpu.VMEM((3 * OFFS, TILES * TILE), bf16),
            pltpu.VMEM((2, 4 * TILE, TILE), bf16),
            pltpu.VMEM((TILES * TILE, 3 * OFFS), bf16),
            pltpu.VMEM((slots, traces), bf16),
            pltpu.VMEM((slots, traces), bf16),
            pltpu.VMEM((slots, samples), bf16),
            pltpu.VMEM((slots, samples), bf16),
            pltpu.VMEM((slots, samples), bf16),
            pltpu.VMEM((slots, samples), bf16),
            pltpu.VMEM((traces, samples), f32),
            pltpu.VMEM((traces, samples), f32),
            pltpu.VMEM((traces, samples), f32),
            pltpu.VMEM((samples + 16, cells), f32),
            pltpu.VMEM(((span + 12) * BLK, cells), f32),
            pltpu.VMEM((2, (span + 14) * BLK, 3 * OFFS), bf16),
            pltpu.VMEM(((span + 14) * BLK, TILES * TILE), bf16),
            pltpu.VMEM((2, (span + 6) * BLK, 3 * OFFS), f32),
            pltpu.VMEM((span * BLK, cells), f32),
            pltpu.VMEM((8, 128), f32),
            pltpu.VMEM((8 * owners, 128), f32),
            dma((2,)),
            dma,
            dma,
            dma((count,)),
            dma((count,)),
            dma((count,)),
            dma((count,)),
            dma,
            dma,
        ],
        compiler_params=pltpu.CompilerParams(
            collective_id=0, has_side_effects=True, vmem_limit_bytes=56 * 1024 * 1024
        ),
        name="exchange_filter",
    )(
        predicted,
        bin_ids.reshape(1, traces),
        offset_slots.reshape(1, traces),
        observed,
        data_weight,
        conv_in,
        conv_mid.reshape(9 * CHAN, CHAN),
        conv_out,
    )


def local(*args):
    traces = args[0].shape[0]
    owners = lax.axis_size("bin")
    if traces // OFFS * (traces // owners) % 16 == 0:
        return fused(*args)
    return by_ops(*args)


def solution(mesh):
    in_specs = (
        P(("line", "bin"), None),
        P(("line", "bin"), None),
        P(("line", "bin"), None),
        P(("line", "bin")),
        P(("line", "bin")),
        P(),
        P(),
        P(),
    )
    out_specs = P(("line", "bin"), None)
    return jax.shard_map(local, mesh=mesh, in_specs=in_specs, out_specs=out_specs, check_vma=False)
```

```python
import jax
import jax.numpy as jnp
from jax import lax
from jax.experimental import pallas as pl
from jax.experimental.pallas import tpu as pltpu
from jax.sharding import PartitionSpec as P

OFFS = 64
CHAN = 48
SEGS = 16
MOST = 46
TILE = 256
CUTS = (4, 13)
BLK = 8
CELLS = TILE // CHAN
SPARE = TILE - CELLS * CHAN
TILES = -(-OFFS // CELLS)
SPLIT_TILE = OFFS // 2 // CELLS
SPLIT = OFFS // 2 % CELLS


def kernel_body(
    span,
    chunk_a,
    chunk_b,
    panel_ref,
    w_in_ref,
    w_mid_ref,
    w_out_ref,
    out_ref,
    ext_ref,
    p3_ref,
    h1_ref,
    z_ref,
):
    blk = SEGS
    n_first = (span + 10) * blk
    n_second = (span + 2) * blk
    for seg in range(SEGS):
        ext_ref[pl.ds(6 * blk + seg, span, stride=blk), :] = panel_ref[
            pl.ds(seg * span, span), :
        ].astype(jnp.float32)
    edge = jnp.zeros((1, OFFS), jnp.float32)
    for b in range(6):
        ext_ref[pl.ds(b * blk, 1), :] = edge
        ext_ref[pl.ds(b * blk + 1, blk - 1), :] = ext_ref[pl.ds((b + span) * blk, blk - 1), :]
        last = (span + 6 + b) * blk
        ext_ref[pl.ds(last, blk - 1), :] = ext_ref[pl.ds((6 + b) * blk + 1, blk - 1), :]
        ext_ref[pl.ds(last + blk - 1, 1), :] = edge
    for tap in range(3):
        p3_ref[:, pl.ds(tap * OFFS, OFFS)] = ext_ref[pl.ds(tap * blk, n_first), :].astype(
            jnp.bfloat16
        )
    @pl.loop(0, n_first // chunk_a)
    def _(step):
        rows = pl.ds(pl.multiple_of(step * chunk_a, 16), chunk_a)
        window = p3_ref[rows, :]
        for tile in range(TILES):
            lanes = pl.ds(tile * TILE, TILE)
            half = jnp.dot(window, w_in_ref[:, lanes], preferred_element_type=jnp.float32)
            h1_ref[rows, lanes] = (half + half * jnp.tanh(half)).astype(jnp.bfloat16)

    seg = lax.broadcasted_iota(jnp.int32, (blk, 1), 0)
    for b in range(5):
        head = pl.ds(b * blk, blk)
        h1_ref[head, :] = jnp.where(seg == 0, 0.0, h1_ref[head, :].astype(jnp.float32)).astype(
            jnp.bfloat16
        )
        tail = pl.ds((span + 5 + b) * blk, blk)
        h1_ref[tail, :] = jnp.where(
            seg == SEGS - 1, 0.0, h1_ref[tail, :].astype(jnp.float32)
        ).astype(jnp.bfloat16)

    @pl.loop(0, n_second // chunk_b)
    def _(step):
        base = pl.multiple_of(step * chunk_b, 16)
        total = jnp.zeros((chunk_b, 3 * OFFS), jnp.float32)
        for tile in range(TILES):
            rows, first = middle_rows(h1_ref, base, chunk_b, tile, blk)
            half = jnp.dot(
                rows,
                w_mid_ref[1 if tile == SPLIT_TILE else 0],
                preferred_element_type=jnp.float32,
            )
            second = first.astype(jnp.float32) + (half + half * jnp.tanh(half))
            total = total + jnp.dot(
                second.astype(jnp.bfloat16),
                w_out_ref[pl.ds(tile * TILE, TILE), :],
                preferred_element_type=jnp.float32,
            )
        z_ref[pl.ds(base, chunk_b), :] = total

    z_ref[pl.ds(0, blk), :] = jnp.where(seg == 0, 0.0, z_ref[pl.ds(0, blk), :])
    last = pl.ds((span + 1) * blk, blk)
    z_ref[last, :] = jnp.where(seg == SEGS - 1, 0.0, z_ref[last, :])

    n_out = span * blk

    @pl.loop(0, 8)
    def _(step):
        size = n_out // 8
        base = pl.multiple_of(step * size, 16)
        left = z_ref[pl.ds(base, size), :][:, 0:OFFS]
        mid = z_ref[pl.ds(base + blk, size), :][:, OFFS : 2 * OFFS]
        right = z_ref[pl.ds(base + 2 * blk, size), :][:, 2 * OFFS : 3 * OFFS]
        centre = p3_ref[pl.ds(base + 5 * blk, size), :].astype(jnp.float32)[:, OFFS : 2 * OFFS]
        ext_ref[pl.ds(base, size), :] = centre + (left + mid + right)

    for seg in range(SEGS):
        out_ref[pl.ds(seg * span, span), :] = ext_ref[
            pl.ds(seg, span, stride=blk), :
        ].astype(jnp.bfloat16)


def largest_chunk(blocks, most):
    return max(d for d in range(1, most + 1) if blocks % d == 0)


def by_chan(v):
    return (v * 43691) >> 21


def one_hot(hit, value):
    return jnp.where(hit, value, 0.0).astype(jnp.bfloat16)


def column(conv_out_ref, a, d):
    row = lax.broadcasted_iota(jnp.int32, (CHAN, CHAN), 0)
    lane = lax.broadcasted_iota(jnp.int32, (CHAN, CHAN), 1)
    taps = jnp.where(row == lane, conv_out_ref[a, d : d + 1, :].astype(jnp.float32), 0.0)
    return jnp.sum(taps, axis=1, keepdims=True)


def weights_body(conv_in_ref, conv_mid_ref, conv_out_ref, w_in_ref, w_mid_ref, w_out_ref):
    f32 = jnp.float32

    def iota(shape, axis):
        return lax.broadcasted_iota(jnp.int32, shape, axis)

    def offset_of(place):
        return jnp.where(place < OFFS // 2, 2 * place, 2 * place - OFFS + 1)

    def cell_of(lane):
        cell = by_chan(lane)
        spare = cell >= CELLS
        return jnp.where(spare, -1, cell), jnp.where(spare, lane - CELLS * CHAN, lane - CHAN * cell)

    others = iota((OFFS, 1), 0) + 1
    chan_down = iota((CHAN, 1), 0)
    chan_across = iota((1, CHAN), 1)

    slot_in, chan_in = cell_of(iota((1, TILE), 1))
    spread = one_hot(chan_in == chan_down, 0.5)
    wide_in = [jnp.dot(conv_in_ref[a], spread, preferred_element_type=f32) for a in range(3)]

    @pl.loop(0, TILES)
    def _(tile):
        base = pl.multiple_of(tile * TILE, TILE)
        near = others - offset_of(slot_in + CELLS * tile)
        for d in range(3):
            value = jnp.zeros((OFFS, TILE), f32)
            for a in range(3):
                value = jnp.where(near == a, wide_in[a][d : d + 1, :], value)
            w_in_ref[pl.ds(d * OFFS, OFFS), pl.ds(base, TILE)] = value.astype(jnp.bfloat16)

    y = iota((1, TILE), 1)
    slot_y = by_chan(y)
    spread_y = one_hot((y - CHAN * slot_y == chan_down) & (slot_y < CELLS), 0.5)
    wide = jnp.dot(conv_mid_ref[...], spread_y, preferred_element_type=f32)

    def taps_of(a, d):
        start = (a * 3 + d) * CHAN
        return wide[start : start + CHAN, :]

    x = iota((TILE, 1), 0)
    slot_x, chan_x = cell_of(x)
    pick = one_hot(chan_x == chan_across, 1.0)
    step = slot_x - slot_y + 1
    apart = (slot_x < SPLIT) != (slot_y < SPLIT)
    for d in range(3):
        value = jnp.zeros((TILE, TILE), f32)
        for a in range(3):
            part = jnp.dot(pick, taps_of(a, d).astype(jnp.bfloat16), preferred_element_type=f32)
            value = jnp.where(step == a, part, value)
        w_mid_ref[0, pl.ds(d * TILE, TILE), :] = value.astype(jnp.bfloat16)
        w_mid_ref[1, pl.ds(d * TILE, TILE), :] = jnp.where(
            apart & (slot_x >= 0), 0.0, value
        ).astype(jnp.bfloat16)
    edge = jnp.zeros((TILE, TILE), f32)
    for d, right, left in ((0, 0, 80), (1, 128, 48), (2, 176, 224)):
        from_right = one_hot((x - right == chan_across) & (x < right + CHAN), 1.0)
        from_left = one_hot(
            (x - left + SPARE == chan_across) & (x >= left) & (x < left + CHAN - SPARE), 1.0
        )
        low = jnp.where(slot_y == 0, taps_of(0, d), 0.0).astype(jnp.bfloat16)
        high = jnp.where(slot_y == CELLS - 1, taps_of(2, d), 0.0).astype(jnp.bfloat16)
        edge = edge + jnp.dot(from_right, high, preferred_element_type=f32)
        edge = edge + jnp.dot(from_left, low, preferred_element_type=f32)
    for kind in range(2):
        w_mid_ref[kind, pl.ds(3 * TILE, TILE), :] = edge.astype(jnp.bfloat16)

    triple = iota((1, 3 * OFFS), 1)
    group = triple // OFFS
    wide_out = []
    for a in range(3):
        value = jnp.zeros((CHAN, 3 * OFFS), f32)
        for d in range(3):
            value = jnp.where(group == d, column(conv_out_ref, a, d), value)
        wide_out.append(value.astype(jnp.bfloat16))
    across = one_hot((chan_x == chan_across) & (slot_x >= 0), 1.0)
    parts = [jnp.dot(across, wide_out[a], preferred_element_type=f32) for a in range(3)]

    @pl.loop(0, TILES)
    def _(tile):
        base = pl.multiple_of(tile * TILE, TILE)
        near = offset_of(slot_x + CELLS * tile) + 1 - (triple - OFFS * group)
        value = jnp.zeros((TILE, 3 * OFFS), f32)
        for a in range(3):
            value = jnp.where(near == a, parts[a], value)
        w_out_ref[pl.ds(base, TILE), :] = value.astype(jnp.bfloat16)


def middle_rows(h1_ref, base, chunk, tile, blk):
    lane = lax.broadcasted_iota(jnp.int32, (1, 128), 1)

    def piece(start, width, tap):
        return h1_ref[pl.ds(base + 4 * blk * tap, chunk), pl.ds(start, width)]

    after = min(tile + 1, TILES - 1) * TILE
    right = [piece(after, 128, tap) for tap in range(3)]
    if tile == 0:
        left = [jnp.zeros((chunk, 128), jnp.bfloat16)] * 3
        turned = left
    else:
        left = [piece(tile * TILE - 128, 128, tap) for tap in range(3)]
        turned = [None, pltpu.roll(left[1], 96, 1), pltpu.roll(left[2], 16, 1)]
    low = jnp.where(lane < 48, right[0], jnp.where(lane < 80, turned[1], left[0]))
    high = jnp.where(
        lane < 48, right[1], jnp.where(lane < 96, pltpu.roll(right[2], 48, 1), turned[2])
    )
    whole = [piece(tile * TILE, TILE, tap) for tap in range(3)]
    return jnp.concatenate(whole + [low, high], axis=1), whole[1]


def band_weights(conv_in, conv_mid, conv_out):
    bf16 = jnp.bfloat16
    return pl.pallas_call(
        weights_body,
        out_shape=(
            jax.ShapeDtypeStruct((3 * OFFS, TILES * TILE), bf16),
            jax.ShapeDtypeStruct((2, 4 * TILE, TILE), bf16),
            jax.ShapeDtypeStruct((TILES * TILE, 3 * OFFS), bf16),
        ),
        in_specs=[pl.BlockSpec(memory_space=pltpu.VMEM)] * 3,
        out_specs=[pl.BlockSpec(memory_space=pltpu.VMEM)] * 3,
        compiler_params=pltpu.CompilerParams(vmem_limit_bytes=40 * 1024 * 1024),
        name="band_weights",
    )(conv_in, conv_mid.reshape(9 * CHAN, CHAN), conv_out)


def filter_rows(panel, weights):
    samples, offs = panel.shape
    span = samples // SEGS
    blk = SEGS
    chunk_a = largest_chunk(span + 10, MOST) * blk
    chunk_b = largest_chunk(span + 2, MOST) * blk

    def body(*refs):
        kernel_body(span, chunk_a, chunk_b, *refs)

    return pl.pallas_call(
        body,
        out_shape=jax.ShapeDtypeStruct((span * blk, offs), jnp.bfloat16),
        in_specs=[pl.BlockSpec(memory_space=pltpu.VMEM)] * 4,
        out_specs=pl.BlockSpec(memory_space=pltpu.VMEM),
        scratch_shapes=[
            pltpu.VMEM(((span + 12) * blk, offs), jnp.float32),
            pltpu.VMEM(((span + 10) * blk, 3 * offs), jnp.bfloat16),
            pltpu.VMEM(((span + 10) * blk, TILES * TILE), jnp.bfloat16),
            pltpu.VMEM(((span + 2) * blk, 3 * offs), jnp.float32),
        ],
        compiler_params=pltpu.CompilerParams(vmem_limit_bytes=48 * 1024 * 1024),
        name="panel_filter",
    )(panel, *weights)


def by_ops(predicted, observed, data_weight, bin_ids, offset_slots, conv_in, conv_mid, conv_out):
    tr_dev, samples = predicted.shape
    owners = lax.axis_size("bin")
    bin_dev = tr_dev // OFFS
    capacity = max(1, tr_dev // owners)
    slots = owners * capacity
    row_index = jnp.arange(tr_dev, dtype=jnp.int32)
    earlier = row_index[None, :] < row_index[:, None]
    same_bin = bin_ids[:, None] == bin_ids[None, :]
    position = jnp.sum((same_bin & earlier).astype(jnp.int32), axis=1)
    owner_slot = (bin_ids // bin_dev) * capacity + position
    local_bin = bin_ids % bin_dev
    mark = jnp.broadcast_to((offset_slots + 1).astype(jnp.bfloat16)[:, None], (tr_dev, 128))
    labelled = jnp.concatenate([predicted, mark], axis=1)
    slot_index = jnp.arange(slots, dtype=jnp.int32)
    offsets = jnp.arange(OFFS, dtype=jnp.int32)

    picks = []
    arrivals = []
    for b in range(bin_dev):
        send_slot = jnp.where(local_bin == b, owner_slot, -1)
        pick = (slot_index[:, None] == send_slot[None, :]).astype(jnp.bfloat16)
        outgoing = jnp.dot(pick, labelled, preferred_element_type=jnp.float32)
        outgoing = outgoing.astype(jnp.bfloat16).reshape(owners, capacity, samples + 128)
        if b == 0:
            outgoing, conv_in, conv_mid, conv_out = lax.optimization_barrier(
                (outgoing, conv_in, conv_mid, conv_out)
            )
            weights = band_weights(conv_in, conv_mid, conv_out)
        else:
            outgoing, weights = lax.optimization_barrier((outgoing, weights))
        arrived = lax.all_to_all(outgoing, "bin", split_axis=0, concat_axis=0, tiled=True)
        picks.append(pick)
        arrivals.append(arrived.reshape(slots, samples + 128))

    own_rows = 0.0
    for b in range(bin_dev):
        cell = arrivals[b][:, samples].astype(jnp.int32) - 1
        cell_pick = (cell[:, None] == offsets[None, :]).astype(jnp.bfloat16)
        panel = jnp.einsum(
            "sc,st->tc",
            cell_pick,
            arrivals[b][:, :samples],
            preferred_element_type=jnp.float32,
        ).astype(jnp.bfloat16)
        filtered = filter_rows(panel, weights)
        answer = jnp.einsum("sc,tc->st", cell_pick, filtered, preferred_element_type=jnp.float32)
        answer = answer.astype(jnp.bfloat16).reshape(owners, capacity, samples)
        returned = lax.all_to_all(answer, "bin", split_axis=0, concat_axis=0, tiled=True)
        own_rows = own_rows + jnp.einsum(
            "sr,st->rt",
            picks[b],
            returned.reshape(slots, samples),
            preferred_element_type=jnp.float32,
        )
    misfit = data_weight * (own_rows - observed)
    share = jnp.broadcast_to(jnp.sum(misfit * misfit), (owners, 1, 128))
    shares = lax.all_to_all(share, "bin", split_axis=0, concat_axis=0, tiled=True)
    misfit_total = jnp.sum(shares[:, 0, 0])
    mean_square = misfit_total / (tr_dev * owners * samples)
    return (misfit * lax.rsqrt(mean_square + 1e-05)).astype(jnp.bfloat16)


def steps_for(rows):
    units = rows // 16
    steps = -(-units // MOST)
    return steps, -(-units // steps) * 16


def at(row):
    return row if isinstance(row, int) else pl.multiple_of(row, 16)


def steps_of(count, straight):
    def run(step_body):
        for step in range(count):
            step_body(step)

    return run if straight else pl.loop(0, count)


def gathered_pieces(samples):
    cuts = [0] + [samples * part // 16 for part in CUTS] + [samples]
    return list(zip(cuts[:-1], cuts[1:]))


def span_of(piece):
    return (piece[1] - piece[0]) // BLK


def fused_body(
    owners,
    pred_ref,
    bins_ref,
    offs_ref,
    observed_ref,
    data_weight_ref,
    conv_in_ref,
    conv_mid_ref,
    conv_out_ref,
    out_ref,
    w_in_ref,
    w_mid_ref,
    w_out_ref,
    mark_out_ref,
    mark_in_ref,
    outgoing_ref,
    arrived_ref,
    answer_ref,
    returned_ref,
    seen_ref,
    scale_ref,
    misfit_ref,
    natural_ref,
    ext_ref,
    p3_ref,
    h1_ref,
    z_ref,
    back_ref,
    part_ref,
    parts_ref,
    load_sem,
    mark_send,
    mark_recv,
    out_send,
    out_recv,
    back_send,
    back_recv,
    part_send,
    part_recv,
):
    f32 = jnp.float32
    bf16 = jnp.bfloat16
    traces, samples = pred_ref.shape
    group = traces // OFFS * (traces // owners)
    slots = owners * group
    per_bin = traces // owners
    pieces = gathered_pieces(samples)
    me = lax.axis_index("bin")

    def partner(step):
        return lax.rem(me + step, owners)

    def rows_of(index, size):
        return pl.ds(pl.multiple_of(index * size, size), size)

    def copy_to(step, source, target, size, lanes, sent, got):
        to = partner(step)
        return pltpu.make_async_remote_copy(
            src_ref=source.at[rows_of(to, size), lanes],
            dst_ref=target.at[rows_of(me, size), lanes],
            send_sem=sent,
            recv_sem=got,
            device_id={"bin": to},
            device_id_type=pl.DeviceIdType.MESH,
        )

    def all_of(source, target, size, lanes, sent, got):
        rows = pl.ds(0, (owners - 1) * size)
        return pltpu.make_async_remote_copy(
            src_ref=source.at[rows, lanes],
            dst_ref=target.at[rows, lanes],
            send_sem=sent,
            recv_sem=got,
            device_id={"bin": partner(1)},
            device_id_type=pl.DeviceIdType.MESH,
        )

    def start(*what):
        @pl.loop(1, owners)
        def _(step):
            copy_to(step, *what).start()

    def wait_recv(*what):
        all_of(*what).wait_recv()

    def wait_send(*what):
        all_of(*what).wait_send()

    loads = [
        pltpu.make_async_copy(observed_ref, seen_ref, load_sem.at[0]),
        pltpu.make_async_copy(data_weight_ref, scale_ref, load_sem.at[1]),
    ]
    for load in loads:
        load.start()

    barrier = pltpu.get_barrier_semaphore()

    @pl.loop(1, owners)
    def _(step):
        pl.semaphore_signal(
            barrier, inc=1, device_id={"bin": partner(step)}, device_id_type=pl.DeviceIdType.MESH
        )

    def iota(shape, axis):
        return lax.broadcasted_iota(jnp.int32, shape, axis)

    wide = jnp.broadcast_to(bins_ref[...], (traces, traces)).astype(f32)
    tall = wide.T
    same = wide == tall
    above = iota((traces, traces), 0)
    beside = iota((traces, traces), 1)
    slot_row = wide[0:1, :] * per_bin + jnp.sum(
        jnp.where(same & (above < beside), 1.0, 0.0), axis=0, keepdims=True
    )
    slot_col = tall[:, 0:1] * per_bin + jnp.sum(
        jnp.where(same & (beside < above), 1.0, 0.0), axis=1, keepdims=True
    )
    pick = jnp.where(iota((slots, 1), 0).astype(f32) == slot_row, 1.0, 0.0).astype(bf16)
    pick_back = jnp.where(slot_col == iota((1, slots), 1).astype(f32), 1.0, 0.0).astype(bf16)
    mark = jnp.broadcast_to(offs_ref[...] + 1, (traces, traces)).astype(f32).T.astype(bf16)
    mark_out_ref[...] = jnp.dot(pick, mark, preferred_element_type=f32).astype(bf16)

    all_marks = (mark_out_ref, mark_in_ref, group, pl.ds(0, traces), mark_send, mark_recv)

    def forward(index):
        low = 0 if index == 0 else pieces[index][0] + 128
        high = samples if index == len(pieces) - 1 else pieces[index][1] + 128
        return low, high

    def forward_copy(index):
        low, high = forward(index)
        return (
            outgoing_ref,
            arrived_ref,
            group,
            pl.ds(low, high - low),
            out_send.at[index],
            out_recv.at[index],
        )

    def back_copy(index):
        low, high = pieces[index]
        return (
            answer_ref,
            returned_ref,
            group,
            pl.ds(low, high - low),
            back_send.at[index],
            back_recv.at[index],
        )

    def fill(index):
        low, high = forward(index)
        for lane in range(low, high, 128):
            outgoing_ref[:, pl.ds(lane, 128)] = jnp.dot(
                pick, pred_ref[:, pl.ds(lane, 128)], preferred_element_type=f32
            ).astype(bf16)

    mine = rows_of(me, group)
    fill(0)
    pl.semaphore_wait(barrier, owners - 1)
    start(*all_marks)
    start(*forward_copy(0))
    for index in range(1, len(pieces)):
        fill(index)
    mark_in_ref[mine, :] = mark_out_ref[mine, :]
    arrived_ref[mine, :] = outgoing_ref[mine, :]
    weights_body(conv_in_ref, conv_mid_ref, conv_out_ref, w_in_ref, w_mid_ref, w_out_ref)
    cells = 2 * OFFS
    nothing = jnp.zeros((8, cells), f32)
    natural_ref[pl.ds(0, 8), :] = nothing
    natural_ref[pl.ds(samples + 8, 8), :] = nothing

    wait_recv(*all_marks)
    cell = iota((slots, cells), 1)
    row = iota((slots, cells), 0)
    offset = (cell & (OFFS - 1)) + 1
    bin_of_row = lax.rem(row, group) >= per_bin
    bin_of_cell = cell >= OFFS
    hit = (mark_in_ref[...].astype(f32) == offset.astype(f32)) & (bin_of_row == bin_of_cell)
    cell_pick_wide = jnp.where(hit, 1.0, 0.0)
    cell_pick = cell_pick_wide.astype(bf16)
    cell_pick_back = cell_pick_wide.T.astype(bf16)

    blk = BLK

    def mask_rows(ref, first_row, count, outside):
        rows = pl.ds(first_row, count)
        row = iota((count, 1), 0)
        ref[rows, :] = jnp.where(outside(row), 0.0, ref[rows, :].astype(f32)).astype(ref.dtype)

    def before(row):
        return ((row & (blk - 1)) == 0) & (row < 5 * blk)

    def behind(row):
        return ((row & (blk - 1)) == blk - 1) & (row >= blk)

    total = jnp.zeros((8, 128), f32)
    for index, piece in enumerate(pieces):
        span = span_of(piece)
        at_start = index == 0
        at_end = index == len(pieces) - 1
        n_first = (span + 10) * blk
        n_second = (span + 2) * blk
        n_out = span * blk
        steps_a, chunk_a = steps_for(n_first)
        steps_b, chunk_b = steps_for(n_second)
        wait_recv(*forward_copy(index))
        if not at_end:
            start(*forward_copy(index + 1))
        for lane in range(*forward(index), 128):
            natural_ref[pl.ds(8 + lane, 128), :] = jnp.dot(
                cell_pick_back, arrived_ref[:, pl.ds(lane, 128)], preferred_element_type=f32
            ).T
        for seg in range(BLK):
            ext_ref[pl.ds(seg, span + 12, stride=blk), :] = natural_ref[
                pl.ds(piece[0] + seg * span + 2, span + 12), :
            ]
        for which in range(2):
            for tap in range(3):
                p3_ref[which, pl.ds(0, n_first), pl.ds(tap * OFFS, OFFS)] = ext_ref[
                    pl.ds(tap * blk, n_first), :
                ][:, which * OFFS : (which + 1) * OFFS].astype(bf16)

        @steps_of(2, steps_a == 1 and steps_b == 1)
        def _(which):
            @steps_of(steps_a, steps_a == 1)
            def _(step):
                rows = pl.ds(at(step * chunk_a), chunk_a)
                window = p3_ref[which, rows, :]
                for tile in range(TILES):
                    lanes = pl.ds(tile * TILE, TILE)
                    half = jnp.dot(window, w_in_ref[:, lanes], preferred_element_type=f32)
                    h1_ref[rows, lanes] = (half + half * jnp.tanh(half)).astype(bf16)

            if at_start:
                mask_rows(h1_ref, 0, 6 * blk, before)
            if at_end:
                mask_rows(h1_ref, (span + 4) * blk, 6 * blk, behind)

            @steps_of(steps_b, steps_b == 1)
            def _(step):
                base = at(step * chunk_b)
                acc = jnp.zeros((chunk_b, 3 * OFFS), f32)
                for tile in range(TILES):
                    rows, first = middle_rows(h1_ref, base, chunk_b, tile, blk)
                    half = jnp.dot(
                        rows,
                        w_mid_ref[1 if tile == SPLIT_TILE else 0],
                        preferred_element_type=f32,
                    )
                    second = first.astype(f32) + (half + half * jnp.tanh(half))
                    acc = acc + jnp.dot(
                        second.astype(bf16),
                        w_out_ref[pl.ds(tile * TILE, TILE), :],
                        preferred_element_type=f32,
                    )
                z_ref[which, pl.ds(base, chunk_b), :] = acc

        for which in range(2):
            if at_start:
                mask_rows(z_ref.at[which], 0, blk, lambda row: row == 0)
            if at_end:
                mask_rows(z_ref.at[which], (span + 1) * blk, blk, lambda row: row == blk - 1)

        @pl.loop(0, 8)
        def _(step):
            size = n_out // 8
            base = pl.multiple_of(step * size, 16)
            sums = []
            for which in range(2):
                left = z_ref[which, pl.ds(base, size), :][:, 0:OFFS]
                mid = z_ref[which, pl.ds(base + blk, size), :][:, OFFS : 2 * OFFS]
                right = z_ref[which, pl.ds(base + 2 * blk, size), :][:, 2 * OFFS : 3 * OFFS]
                sums.append(left + mid + right)
            centre = ext_ref[pl.ds(base + 6 * blk, size), :]
            ext_ref[pl.ds(base, size), :] = centre + jnp.concatenate(sums, axis=1)

        for seg in range(BLK):
            back_ref[pl.ds(seg * span, span), :] = ext_ref[pl.ds(seg, span, stride=blk), :]
        for lane in range(0, n_out, 128):
            answer_ref[:, pl.ds(piece[0] + lane, 128)] = jnp.dot(
                cell_pick,
                back_ref[pl.ds(lane, 128), :].T.astype(bf16),
                preferred_element_type=f32,
            ).astype(bf16)
        start(*back_copy(index))

    returned_ref[mine, :] = answer_ref[mine, :]
    for load in loads:
        load.wait()
    for index, piece in enumerate(pieces):
        wait_recv(*back_copy(index))
        for lane in range(*piece, 128):
            lanes = pl.ds(lane, 128)
            own = jnp.dot(pick_back, returned_ref[:, lanes], preferred_element_type=f32)
            miss = scale_ref[:, lanes] * (own - seen_ref[:, lanes])
            misfit_ref[:, lanes] = miss
            total = total + jnp.sum((miss * miss).reshape(traces // 8, 8, 128), axis=0)

    part_ref[...] = total

    @pl.loop(1, owners)
    def _(step):
        pltpu.make_async_remote_copy(
            src_ref=part_ref,
            dst_ref=parts_ref.at[rows_of(me, 8), :],
            send_sem=part_send,
            recv_sem=part_recv,
            device_id={"bin": partner(step)},
            device_id_type=pl.DeviceIdType.MESH,
        ).start()

    all_parts = (parts_ref, parts_ref, 8, pl.ds(0, 128), part_send, part_recv)
    parts_ref[rows_of(me, 8), :] = total
    wait_recv(*all_parts)
    mean_square = jnp.sum(parts_ref[...], keepdims=True) / (traces * owners * samples)
    out_ref[...] = (misfit_ref[...] * lax.rsqrt(mean_square + 1e-05)).astype(bf16)

    wait_send(*all_parts)
    wait_send(*all_marks)
    for index in range(len(pieces)):
        wait_send(*forward_copy(index))
        wait_send(*back_copy(index))


def fused(predicted, observed, data_weight, bin_ids, offset_slots, conv_in, conv_mid, conv_out):
    traces, samples = predicted.shape
    owners = lax.axis_size("bin")
    group = traces // OFFS * (traces // owners)
    slots = owners * group
    pieces = gathered_pieces(samples)
    count = len(pieces)
    span = max(span_of(piece) for piece in pieces)
    cells = 2 * OFFS
    bf16 = jnp.bfloat16
    f32 = jnp.float32
    dma = pltpu.SemaphoreType.DMA
    vmem = pl.BlockSpec(memory_space=pltpu.VMEM)
    anywhere = pl.BlockSpec(memory_space=pl.ANY)

    def body(*refs):
        fused_body(owners, *refs)

    return pl.pallas_call(
        body,
        out_shape=jax.ShapeDtypeStruct((traces, samples), bf16),
        in_specs=[vmem, vmem, vmem, anywhere, anywhere, vmem, vmem, vmem],
        out_specs=vmem,
        scratch_shapes=[
            pltpu.VMEM((3 * OFFS, TILES * TILE), bf16),
            pltpu.VMEM((2, 4 * TILE, TILE), bf16),
            pltpu.VMEM((TILES * TILE, 3 * OFFS), bf16),
            pltpu.VMEM((slots, traces), bf16),
            pltpu.VMEM((slots, traces), bf16),
            pltpu.VMEM((slots, samples), bf16),
            pltpu.VMEM((slots, samples), bf16),
            pltpu.VMEM((slots, samples), bf16),
            pltpu.VMEM((slots, samples), bf16),
            pltpu.VMEM((traces, samples), f32),
            pltpu.VMEM((traces, samples), f32),
            pltpu.VMEM((traces, samples), f32),
            pltpu.VMEM((samples + 16, cells), f32),
            pltpu.VMEM(((span + 12) * BLK, cells), f32),
            pltpu.VMEM((2, (span + 14) * BLK, 3 * OFFS), bf16),
            pltpu.VMEM(((span + 14) * BLK, TILES * TILE), bf16),
            pltpu.VMEM((2, (span + 6) * BLK, 3 * OFFS), f32),
            pltpu.VMEM((span * BLK, cells), f32),
            pltpu.VMEM((8, 128), f32),
            pltpu.VMEM((8 * owners, 128), f32),
            dma((2,)),
            dma,
            dma,
            dma((count,)),
            dma((count,)),
            dma((count,)),
            dma((count,)),
            dma,
            dma,
        ],
        compiler_params=pltpu.CompilerParams(
            collective_id=0, has_side_effects=True, vmem_limit_bytes=56 * 1024 * 1024
        ),
        name="exchange_filter",
    )(
        predicted,
        bin_ids.reshape(1, traces),
        offset_slots.reshape(1, traces),
        observed,
        data_weight,
        conv_in,
        conv_mid.reshape(9 * CHAN, CHAN),
        conv_out,
    )


def local(*args):
    traces = args[0].shape[0]
    owners = lax.axis_size("bin")
    if traces // OFFS * (traces // owners) % 16 == 0:
        return fused(*args)
    return by_ops(*args)


def solution(mesh):
    in_specs = (
        P(("line", "bin"), None),
        P(("line", "bin"), None),
        P(("line", "bin"), None),
        P(("line", "bin")),
        P(("line", "bin")),
        P(),
        P(),
        P(),
    )
    out_specs = P(("line", "bin"), None)
    return jax.shard_map(local, mesh=mesh, in_specs=in_specs, out_specs=out_specs, check_vma=False)
```

```python
import jax
import jax.numpy as jnp
from jax import lax
from jax.experimental import pallas as pl
from jax.experimental.pallas import tpu as pltpu
from jax.sharding import PartitionSpec as P

OFFS = 64
CHAN = 48
SEGS = 16
MOST = 46
TILE = 256
CUTS = (4, 13)
BLK = 8
CELLS = TILE // CHAN
SPARE = TILE - CELLS * CHAN
TILES = -(-OFFS // CELLS)
SPLIT_TILE = OFFS // 2 // CELLS
SPLIT = OFFS // 2 % CELLS


def kernel_body(
    span,
    chunk_a,
    chunk_b,
    panel_ref,
    w_in_ref,
    w_mid_ref,
    w_out_ref,
    out_ref,
    ext_ref,
    p3_ref,
    h1_ref,
    z_ref,
):
    blk = SEGS
    n_first = (span + 10) * blk
    n_second = (span + 2) * blk
    for seg in range(SEGS):
        ext_ref[pl.ds(6 * blk + seg, span, stride=blk), :] = panel_ref[
            pl.ds(seg * span, span), :
        ].astype(jnp.float32)
    edge = jnp.zeros((1, OFFS), jnp.float32)
    for b in range(6):
        ext_ref[pl.ds(b * blk, 1), :] = edge
        ext_ref[pl.ds(b * blk + 1, blk - 1), :] = ext_ref[pl.ds((b + span) * blk, blk - 1), :]
        last = (span + 6 + b) * blk
        ext_ref[pl.ds(last, blk - 1), :] = ext_ref[pl.ds((6 + b) * blk + 1, blk - 1), :]
        ext_ref[pl.ds(last + blk - 1, 1), :] = edge
    for tap in range(3):
        p3_ref[:, pl.ds(tap * OFFS, OFFS)] = ext_ref[pl.ds(tap * blk, n_first), :].astype(
            jnp.bfloat16
        )
    @pl.loop(0, n_first // chunk_a)
    def _(step):
        rows = pl.ds(pl.multiple_of(step * chunk_a, 16), chunk_a)
        window = p3_ref[rows, :]
        for tile in range(TILES):
            lanes = pl.ds(tile * TILE, TILE)
            half = jnp.dot(window, w_in_ref[:, lanes], preferred_element_type=jnp.float32)
            h1_ref[rows, lanes] = (half + half * jnp.tanh(half)).astype(jnp.bfloat16)

    seg = lax.broadcasted_iota(jnp.int32, (blk, 1), 0)
    for b in range(5):
        head = pl.ds(b * blk, blk)
        h1_ref[head, :] = jnp.where(seg == 0, 0.0, h1_ref[head, :].astype(jnp.float32)).astype(
            jnp.bfloat16
        )
        tail = pl.ds((span + 5 + b) * blk, blk)
        h1_ref[tail, :] = jnp.where(
            seg == SEGS - 1, 0.0, h1_ref[tail, :].astype(jnp.float32)
        ).astype(jnp.bfloat16)

    @pl.loop(0, n_second // chunk_b)
    def _(step):
        base = pl.multiple_of(step * chunk_b, 16)
        total = jnp.zeros((chunk_b, 3 * OFFS), jnp.float32)
        for tile in range(TILES):
            rows, first = middle_rows(h1_ref, base, chunk_b, tile, blk)
            half = jnp.dot(
                rows,
                w_mid_ref[1 if tile == SPLIT_TILE else 0],
                preferred_element_type=jnp.float32,
            )
            second = first.astype(jnp.float32) + (half + half * jnp.tanh(half))
            total = total + jnp.dot(
                second.astype(jnp.bfloat16),
                w_out_ref[pl.ds(tile * TILE, TILE), :],
                preferred_element_type=jnp.float32,
            )
        z_ref[pl.ds(base, chunk_b), :] = total

    z_ref[pl.ds(0, blk), :] = jnp.where(seg == 0, 0.0, z_ref[pl.ds(0, blk), :])
    last = pl.ds((span + 1) * blk, blk)
    z_ref[last, :] = jnp.where(seg == SEGS - 1, 0.0, z_ref[last, :])

    n_out = span * blk

    @pl.loop(0, 8)
    def _(step):
        size = n_out // 8
        base = pl.multiple_of(step * size, 16)
        left = z_ref[pl.ds(base, size), :][:, 0:OFFS]
        mid = z_ref[pl.ds(base + blk, size), :][:, OFFS : 2 * OFFS]
        right = z_ref[pl.ds(base + 2 * blk, size), :][:, 2 * OFFS : 3 * OFFS]
        centre = p3_ref[pl.ds(base + 5 * blk, size), :].astype(jnp.float32)[:, OFFS : 2 * OFFS]
        ext_ref[pl.ds(base, size), :] = centre + (left + mid + right)

    for seg in range(SEGS):
        out_ref[pl.ds(seg * span, span), :] = ext_ref[
            pl.ds(seg, span, stride=blk), :
        ].astype(jnp.bfloat16)


def largest_chunk(blocks, most):
    return max(d for d in range(1, most + 1) if blocks % d == 0)


def by_chan(v):
    return (v * 43691) >> 21


def one_hot(hit, value):
    return jnp.where(hit, value, 0.0).astype(jnp.bfloat16)


def column(conv_out_ref, a, d):
    row = lax.broadcasted_iota(jnp.int32, (CHAN, CHAN), 0)
    lane = lax.broadcasted_iota(jnp.int32, (CHAN, CHAN), 1)
    taps = jnp.where(row == lane, conv_out_ref[a, d : d + 1, :].astype(jnp.float32), 0.0)
    return jnp.sum(taps, axis=1, keepdims=True)


def weights_body(conv_in_ref, conv_mid_ref, conv_out_ref, w_in_ref, w_mid_ref, w_out_ref):
    f32 = jnp.float32

    def iota(shape, axis):
        return lax.broadcasted_iota(jnp.int32, shape, axis)

    def offset_of(place):
        return jnp.where(place < OFFS // 2, 2 * place, 2 * place - OFFS + 1)

    def cell_of(lane):
        cell = by_chan(lane)
        spare = cell >= CELLS
        return jnp.where(spare, -1, cell), jnp.where(spare, lane - CELLS * CHAN, lane - CHAN * cell)

    others = iota((OFFS, 1), 0) + 1
    chan_down = iota((CHAN, 1), 0)
    chan_across = iota((1, CHAN), 1)

    slot_in, chan_in = cell_of(iota((1, TILE), 1))
    spread = one_hot(chan_in == chan_down, 0.5)
    wide_in = [jnp.dot(conv_in_ref[a], spread, preferred_element_type=f32) for a in range(3)]

    @pl.loop(0, TILES)
    def _(tile):
        base = pl.multiple_of(tile * TILE, TILE)
        near = others - offset_of(slot_in + CELLS * tile)
        for d in range(3):
            value = jnp.zeros((OFFS, TILE), f32)
            for a in range(3):
                value = jnp.where(near == a, wide_in[a][d : d + 1, :], value)
            w_in_ref[pl.ds(d * OFFS, OFFS), pl.ds(base, TILE)] = value.astype(jnp.bfloat16)

    y = iota((1, TILE), 1)
    slot_y = by_chan(y)
    spread_y = one_hot((y - CHAN * slot_y == chan_down) & (slot_y < CELLS), 0.5)
    wide = jnp.dot(conv_mid_ref[...], spread_y, preferred_element_type=f32)

    def taps_of(a, d):
        start = (a * 3 + d) * CHAN
        return wide[start : start + CHAN, :]

    x = iota((TILE, 1), 0)
    slot_x, chan_x = cell_of(x)
    pick = one_hot(chan_x == chan_across, 1.0)
    step = slot_x - slot_y + 1
    apart = (slot_x < SPLIT) != (slot_y < SPLIT)
    for d in range(3):
        value = jnp.zeros((TILE, TILE), f32)
        for a in range(3):
            part = jnp.dot(pick, taps_of(a, d).astype(jnp.bfloat16), preferred_element_type=f32)
            value = jnp.where(step == a, part, value)
        w_mid_ref[0, pl.ds(d * TILE, TILE), :] = value.astype(jnp.bfloat16)
        w_mid_ref[1, pl.ds(d * TILE, TILE), :] = jnp.where(
            apart & (slot_x >= 0), 0.0, value
        ).astype(jnp.bfloat16)
    edge = jnp.zeros((TILE, TILE), f32)
    for d, right, left in ((0, 0, 80), (1, 128, 48), (2, 176, 224)):
        from_right = one_hot((x - right == chan_across) & (x < right + CHAN), 1.0)
        from_left = one_hot(
            (x - left + SPARE == chan_across) & (x >= left) & (x < left + CHAN - SPARE), 1.0
        )
        low = jnp.where(slot_y == 0, taps_of(0, d), 0.0).astype(jnp.bfloat16)
        high = jnp.where(slot_y == CELLS - 1, taps_of(2, d), 0.0).astype(jnp.bfloat16)
        edge = edge + jnp.dot(from_right, high, preferred_element_type=f32)
        edge = edge + jnp.dot(from_left, low, preferred_element_type=f32)
    for kind in range(2):
        w_mid_ref[kind, pl.ds(3 * TILE, TILE), :] = edge.astype(jnp.bfloat16)

    triple = iota((1, 3 * OFFS), 1)
    group = triple // OFFS
    wide_out = []
    for a in range(3):
        value = jnp.zeros((CHAN, 3 * OFFS), f32)
        for d in range(3):
            value = jnp.where(group == d, column(conv_out_ref, a, d), value)
        wide_out.append(value.astype(jnp.bfloat16))
    across = one_hot((chan_x == chan_across) & (slot_x >= 0), 1.0)
    parts = [jnp.dot(across, wide_out[a], preferred_element_type=f32) for a in range(3)]

    @pl.loop(0, TILES)
    def _(tile):
        base = pl.multiple_of(tile * TILE, TILE)
        near = offset_of(slot_x + CELLS * tile) + 1 - (triple - OFFS * group)
        value = jnp.zeros((TILE, 3 * OFFS), f32)
        for a in range(3):
            value = jnp.where(near == a, parts[a], value)
        w_out_ref[pl.ds(base, TILE), :] = value.astype(jnp.bfloat16)


def middle_rows(h1_ref, base, chunk, tile, blk):
    lane = lax.broadcasted_iota(jnp.int32, (1, 128), 1)

    def piece(start, width, tap):
        return h1_ref[pl.ds(base + 4 * blk * tap, chunk), pl.ds(start, width)]

    after = min(tile + 1, TILES - 1) * TILE
    right = [piece(after, 128, tap) for tap in range(3)]
    if tile == 0:
        left = [jnp.zeros((chunk, 128), jnp.bfloat16)] * 3
        turned = left
    else:
        left = [piece(tile * TILE - 128, 128, tap) for tap in range(3)]
        turned = [None, pltpu.roll(left[1], 96, 1), pltpu.roll(left[2], 16, 1)]
    low = jnp.where(lane < 48, right[0], jnp.where(lane < 80, turned[1], left[0]))
    high = jnp.where(
        lane < 48, right[1], jnp.where(lane < 96, pltpu.roll(right[2], 48, 1), turned[2])
    )
    whole = [piece(tile * TILE, TILE, tap) for tap in range(3)]
    return jnp.concatenate(whole + [low, high], axis=1), whole[1]


def band_weights(conv_in, conv_mid, conv_out):
    bf16 = jnp.bfloat16
    return pl.pallas_call(
        weights_body,
        out_shape=(
            jax.ShapeDtypeStruct((3 * OFFS, TILES * TILE), bf16),
            jax.ShapeDtypeStruct((2, 4 * TILE, TILE), bf16),
            jax.ShapeDtypeStruct((TILES * TILE, 3 * OFFS), bf16),
        ),
        in_specs=[pl.BlockSpec(memory_space=pltpu.VMEM)] * 3,
        out_specs=[pl.BlockSpec(memory_space=pltpu.VMEM)] * 3,
        compiler_params=pltpu.CompilerParams(vmem_limit_bytes=40 * 1024 * 1024),
        name="band_weights",
    )(conv_in, conv_mid.reshape(9 * CHAN, CHAN), conv_out)


def filter_rows(panel, weights):
    samples, offs = panel.shape
    span = samples // SEGS
    blk = SEGS
    chunk_a = largest_chunk(span + 10, MOST) * blk
    chunk_b = largest_chunk(span + 2, MOST) * blk

    def body(*refs):
        kernel_body(span, chunk_a, chunk_b, *refs)

    return pl.pallas_call(
        body,
        out_shape=jax.ShapeDtypeStruct((span * blk, offs), jnp.bfloat16),
        in_specs=[pl.BlockSpec(memory_space=pltpu.VMEM)] * 4,
        out_specs=pl.BlockSpec(memory_space=pltpu.VMEM),
        scratch_shapes=[
            pltpu.VMEM(((span + 12) * blk, offs), jnp.float32),
            pltpu.VMEM(((span + 10) * blk, 3 * offs), jnp.bfloat16),
            pltpu.VMEM(((span + 10) * blk, TILES * TILE), jnp.bfloat16),
            pltpu.VMEM(((span + 2) * blk, 3 * offs), jnp.float32),
        ],
        compiler_params=pltpu.CompilerParams(vmem_limit_bytes=48 * 1024 * 1024),
        name="panel_filter",
    )(panel, *weights)


def by_ops(predicted, observed, data_weight, bin_ids, offset_slots, conv_in, conv_mid, conv_out):
    tr_dev, samples = predicted.shape
    owners = lax.axis_size("bin")
    bin_dev = tr_dev // OFFS
    capacity = max(1, tr_dev // owners)
    slots = owners * capacity
    row_index = jnp.arange(tr_dev, dtype=jnp.int32)
    earlier = row_index[None, :] < row_index[:, None]
    same_bin = bin_ids[:, None] == bin_ids[None, :]
    position = jnp.sum((same_bin & earlier).astype(jnp.int32), axis=1)
    owner_slot = (bin_ids // bin_dev) * capacity + position
    local_bin = bin_ids % bin_dev
    mark = jnp.broadcast_to((offset_slots + 1).astype(jnp.bfloat16)[:, None], (tr_dev, 128))
    labelled = jnp.concatenate([predicted, mark], axis=1)
    slot_index = jnp.arange(slots, dtype=jnp.int32)
    offsets = jnp.arange(OFFS, dtype=jnp.int32)

    picks = []
    arrivals = []
    for b in range(bin_dev):
        send_slot = jnp.where(local_bin == b, owner_slot, -1)
        pick = (slot_index[:, None] == send_slot[None, :]).astype(jnp.bfloat16)
        outgoing = jnp.dot(pick, labelled, preferred_element_type=jnp.float32)
        outgoing = outgoing.astype(jnp.bfloat16).reshape(owners, capacity, samples + 128)
        if b == 0:
            outgoing, conv_in, conv_mid, conv_out = lax.optimization_barrier(
                (outgoing, conv_in, conv_mid, conv_out)
            )
            weights = band_weights(conv_in, conv_mid, conv_out)
        else:
            outgoing, weights = lax.optimization_barrier((outgoing, weights))
        arrived = lax.all_to_all(outgoing, "bin", split_axis=0, concat_axis=0, tiled=True)
        picks.append(pick)
        arrivals.append(arrived.reshape(slots, samples + 128))

    own_rows = 0.0
    for b in range(bin_dev):
        cell = arrivals[b][:, samples].astype(jnp.int32) - 1
        cell_pick = (cell[:, None] == offsets[None, :]).astype(jnp.bfloat16)
        panel = jnp.einsum(
            "sc,st->tc",
            cell_pick,
            arrivals[b][:, :samples],
            preferred_element_type=jnp.float32,
        ).astype(jnp.bfloat16)
        filtered = filter_rows(panel, weights)
        answer = jnp.einsum("sc,tc->st", cell_pick, filtered, preferred_element_type=jnp.float32)
        answer = answer.astype(jnp.bfloat16).reshape(owners, capacity, samples)
        returned = lax.all_to_all(answer, "bin", split_axis=0, concat_axis=0, tiled=True)
        own_rows = own_rows + jnp.einsum(
            "sr,st->rt",
            picks[b],
            returned.reshape(slots, samples),
            preferred_element_type=jnp.float32,
        )
    misfit = data_weight * (own_rows - observed)
    share = jnp.broadcast_to(jnp.sum(misfit * misfit), (owners, 1, 128))
    shares = lax.all_to_all(share, "bin", split_axis=0, concat_axis=0, tiled=True)
    misfit_total = jnp.sum(shares[:, 0, 0])
    mean_square = misfit_total / (tr_dev * owners * samples)
    return (misfit * lax.rsqrt(mean_square + 1e-05)).astype(jnp.bfloat16)


def steps_for(rows):
    units = rows // 16
    steps = -(-units // MOST)
    return steps, -(-units // steps) * 16


def at(row):
    return row if isinstance(row, int) else pl.multiple_of(row, 16)


def steps_of(count, straight):
    def run(step_body):
        for step in range(count):
            step_body(step)

    return run if straight else pl.loop(0, count)


def gathered_pieces(samples):
    cuts = [0] + [samples * part // 16 for part in CUTS] + [samples]
    return list(zip(cuts[:-1], cuts[1:]))


def span_of(piece):
    return (piece[1] - piece[0]) // BLK


def fused_body(
    owners,
    pred_ref,
    bins_ref,
    offs_ref,
    observed_ref,
    data_weight_ref,
    conv_in_ref,
    conv_mid_ref,
    conv_out_ref,
    out_ref,
    w_in_ref,
    w_mid_ref,
    w_out_ref,
    mark_out_ref,
    mark_in_ref,
    outgoing_ref,
    arrived_ref,
    answer_ref,
    returned_ref,
    seen_ref,
    scale_ref,
    misfit_ref,
    natural_ref,
    ext_ref,
    p3_ref,
    h1_ref,
    z_ref,
    back_ref,
    part_ref,
    parts_ref,
    load_sem,
    mark_send,
    mark_recv,
    out_send,
    out_recv,
    back_send,
    back_recv,
    part_send,
    part_recv,
):
    f32 = jnp.float32
    bf16 = jnp.bfloat16
    traces, samples = pred_ref.shape
    group = traces // OFFS * (traces // owners)
    slots = owners * group
    per_bin = traces // owners
    pieces = gathered_pieces(samples)
    me = lax.axis_index("bin")

    def partner(step):
        return lax.rem(me + step, owners)

    def rows_of(index, size):
        return pl.ds(pl.multiple_of(index * size, size), size)

    def copy_to(step, source, target, size, lanes, sent, got):
        to = partner(step)
        return pltpu.make_async_remote_copy(
            src_ref=source.at[rows_of(to, size), lanes],
            dst_ref=target.at[rows_of(me, size), lanes],
            send_sem=sent,
            recv_sem=got,
            device_id={"bin": to},
            device_id_type=pl.DeviceIdType.MESH,
        )

    def all_of(source, target, size, lanes, sent, got):
        rows = pl.ds(0, (owners - 1) * size)
        return pltpu.make_async_remote_copy(
            src_ref=source.at[rows, lanes],
            dst_ref=target.at[rows, lanes],
            send_sem=sent,
            recv_sem=got,
            device_id={"bin": partner(1)},
            device_id_type=pl.DeviceIdType.MESH,
        )

    def start(*what):
        @pl.loop(1, owners)
        def _(step):
            copy_to(step, *what).start()

    def wait_recv(*what):
        all_of(*what).wait_recv()

    def wait_send(*what):
        all_of(*what).wait_send()

    loads = [
        pltpu.make_async_copy(observed_ref, seen_ref, load_sem.at[0]),
        pltpu.make_async_copy(data_weight_ref, scale_ref, load_sem.at[1]),
    ]
    for load in loads:
        load.start()

    barrier = pltpu.get_barrier_semaphore()

    @pl.loop(1, owners)
    def _(step):
        pl.semaphore_signal(
            barrier, inc=1, device_id={"bin": partner(step)}, device_id_type=pl.DeviceIdType.MESH
        )

    def iota(shape, axis):
        return lax.broadcasted_iota(jnp.int32, shape, axis)

    wide = jnp.broadcast_to(bins_ref[...], (traces, traces)).astype(f32)
    tall = wide.T
    same = wide == tall
    above = iota((traces, traces), 0)
    beside = iota((traces, traces), 1)
    slot_row = wide[0:1, :] * per_bin + jnp.sum(
        jnp.where(same & (above < beside), 1.0, 0.0), axis=0, keepdims=True
    )
    slot_col = tall[:, 0:1] * per_bin + jnp.sum(
        jnp.where(same & (beside < above), 1.0, 0.0), axis=1, keepdims=True
    )
    pick = jnp.where(iota((slots, 1), 0).astype(f32) == slot_row, 1.0, 0.0).astype(bf16)
    pick_back = jnp.where(slot_col == iota((1, slots), 1).astype(f32), 1.0, 0.0).astype(bf16)
    mark = jnp.broadcast_to(offs_ref[...] + 1, (traces, traces)).astype(f32).T.astype(bf16)
    mark_out_ref[...] = jnp.dot(pick, mark, preferred_element_type=f32).astype(bf16)

    all_marks = (mark_out_ref, mark_in_ref, group, pl.ds(0, traces), mark_send, mark_recv)

    def forward(index):
        low = 0 if index == 0 else pieces[index][0] + 128
        high = samples if index == len(pieces) - 1 else pieces[index][1] + 128
        return low, high

    def forward_copy(index):
        low, high = forward(index)
        return (
            outgoing_ref,
            arrived_ref,
            group,
            pl.ds(low, high - low),
            out_send.at[index],
            out_recv.at[index],
        )

    def back_copy(index):
        low, high = pieces[index]
        return (
            answer_ref,
            returned_ref,
            group,
            pl.ds(low, high - low),
            back_send.at[index],
            back_recv.at[index],
        )

    def fill(index):
        low, high = forward(index)
        for lane in range(low, high, 128):
            outgoing_ref[:, pl.ds(lane, 128)] = jnp.dot(
                pick, pred_ref[:, pl.ds(lane, 128)], preferred_element_type=f32
            ).astype(bf16)

    mine = rows_of(me, group)
    fill(0)
    pl.semaphore_wait(barrier, owners - 1)
    start(*all_marks)
    start(*forward_copy(0))
    for index in range(1, len(pieces)):
        fill(index)
    mark_in_ref[mine, :] = mark_out_ref[mine, :]
    arrived_ref[mine, :] = outgoing_ref[mine, :]
    weights_body(conv_in_ref, conv_mid_ref, conv_out_ref, w_in_ref, w_mid_ref, w_out_ref)
    cells = 2 * OFFS
    nothing = jnp.zeros((8, cells), f32)
    natural_ref[pl.ds(0, 8), :] = nothing
    natural_ref[pl.ds(samples + 8, 8), :] = nothing

    wait_recv(*all_marks)
    cell = iota((slots, cells), 1)
    row = iota((slots, cells), 0)
    offset = (cell & (OFFS - 1)) + 1
    bin_of_row = lax.rem(row, group) >= per_bin
    bin_of_cell = cell >= OFFS
    hit = (mark_in_ref[...].astype(f32) == offset.astype(f32)) & (bin_of_row == bin_of_cell)
    cell_pick_wide = jnp.where(hit, 1.0, 0.0)
    cell_pick = cell_pick_wide.astype(bf16)
    cell_pick_back = cell_pick_wide.T.astype(bf16)

    blk = BLK

    def mask_rows(ref, first_row, count, outside):
        rows = pl.ds(first_row, count)
        row = iota((count, 1), 0)
        ref[rows, :] = jnp.where(outside(row), 0.0, ref[rows, :].astype(f32)).astype(ref.dtype)

    def before(row):
        return ((row & (blk - 1)) == 0) & (row < 5 * blk)

    def behind(row):
        return ((row & (blk - 1)) == blk - 1) & (row >= blk)

    total = jnp.zeros((8, 128), f32)
    for index, piece in enumerate(pieces):
        span = span_of(piece)
        at_start = index == 0
        at_end = index == len(pieces) - 1
        n_first = (span + 10) * blk
        n_second = (span + 2) * blk
        n_out = span * blk
        steps_a, chunk_a = steps_for(n_first)
        steps_b, chunk_b = steps_for(n_second)
        wait_recv(*forward_copy(index))
        if not at_end:
            start(*forward_copy(index + 1))
        for lane in range(*forward(index), 128):
            natural_ref[pl.ds(8 + lane, 128), :] = jnp.dot(
                cell_pick_back, arrived_ref[:, pl.ds(lane, 128)], preferred_element_type=f32
            ).T
        for seg in range(BLK):
            ext_ref[pl.ds(seg, span + 12, stride=blk), :] = natural_ref[
                pl.ds(piece[0] + seg * span + 2, span + 12), :
            ]
        for which in range(2):
            for tap in range(3):
                p3_ref[which, pl.ds(0, n_first), pl.ds(tap * OFFS, OFFS)] = ext_ref[
                    pl.ds(tap * blk, n_first), :
                ][:, which * OFFS : (which + 1) * OFFS].astype(bf16)

        @steps_of(2, steps_a == 1 and steps_b == 1)
        def _(which):
            @steps_of(steps_a, steps_a == 1)
            def _(step):
                rows = pl.ds(at(step * chunk_a), chunk_a)
                window = p3_ref[which, rows, :]
                for tile in range(TILES):
                    lanes = pl.ds(tile * TILE, TILE)
                    half = jnp.dot(window, w_in_ref[:, lanes], preferred_element_type=f32)
                    h1_ref[rows, lanes] = (half + half * jnp.tanh(half)).astype(bf16)

            if at_start:
                mask_rows(h1_ref, 0, 6 * blk, before)
            if at_end:
                mask_rows(h1_ref, (span + 4) * blk, 6 * blk, behind)

            @steps_of(steps_b, steps_b == 1)
            def _(step):
                base = at(step * chunk_b)
                acc = jnp.zeros((chunk_b, 3 * OFFS), f32)
                for tile in range(TILES):
                    rows, first = middle_rows(h1_ref, base, chunk_b, tile, blk)
                    half = jnp.dot(
                        rows,
                        w_mid_ref[1 if tile == SPLIT_TILE else 0],
                        preferred_element_type=f32,
                    )
                    second = first.astype(f32) + (half + half * jnp.tanh(half))
                    acc = acc + jnp.dot(
                        second.astype(bf16),
                        w_out_ref[pl.ds(tile * TILE, TILE), :],
                        preferred_element_type=f32,
                    )
                z_ref[which, pl.ds(base, chunk_b), :] = acc

        for which in range(2):
            if at_start:
                mask_rows(z_ref.at[which], 0, blk, lambda row: row == 0)
            if at_end:
                mask_rows(z_ref.at[which], (span + 1) * blk, blk, lambda row: row == blk - 1)

        @pl.loop(0, 4)
        def _(step):
            size = n_out // 4
            base = pl.multiple_of(step * size, 16)
            sums = []
            for which in range(2):
                left = z_ref[which, pl.ds(base, size), :][:, 0:OFFS]
                mid = z_ref[which, pl.ds(base + blk, size), :][:, OFFS : 2 * OFFS]
                right = z_ref[which, pl.ds(base + 2 * blk, size), :][:, 2 * OFFS : 3 * OFFS]
                sums.append(left + mid + right)
            centre = ext_ref[pl.ds(base + 6 * blk, size), :]
            ext_ref[pl.ds(base, size), :] = centre + jnp.concatenate(sums, axis=1)

        for seg in range(BLK):
            back_ref[pl.ds(seg * span, span), :] = ext_ref[pl.ds(seg, span, stride=blk), :]
        for lane in range(0, n_out, 128):
            answer_ref[:, pl.ds(piece[0] + lane, 128)] = jnp.dot(
                cell_pick,
                back_ref[pl.ds(lane, 128), :].T.astype(bf16),
                preferred_element_type=f32,
            ).astype(bf16)
        start(*back_copy(index))

    returned_ref[mine, :] = answer_ref[mine, :]
    for load in loads:
        load.wait()
    for index, piece in enumerate(pieces):
        wait_recv(*back_copy(index))
        for lane in range(*piece, 128):
            lanes = pl.ds(lane, 128)
            own = jnp.dot(pick_back, returned_ref[:, lanes], preferred_element_type=f32)
            miss = scale_ref[:, lanes] * (own - seen_ref[:, lanes])
            misfit_ref[:, lanes] = miss
            total = total + jnp.sum((miss * miss).reshape(traces // 8, 8, 128), axis=0)

    part_ref[...] = total

    @pl.loop(1, owners)
    def _(step):
        pltpu.make_async_remote_copy(
            src_ref=part_ref,
            dst_ref=parts_ref.at[rows_of(me, 8), :],
            send_sem=part_send,
            recv_sem=part_recv,
            device_id={"bin": partner(step)},
            device_id_type=pl.DeviceIdType.MESH,
        ).start()

    all_parts = (parts_ref, parts_ref, 8, pl.ds(0, 128), part_send, part_recv)
    parts_ref[rows_of(me, 8), :] = total
    wait_recv(*all_parts)
    mean_square = jnp.sum(parts_ref[...], keepdims=True) / (traces * owners * samples)
    out_ref[...] = (misfit_ref[...] * lax.rsqrt(mean_square + 1e-05)).astype(bf16)

    wait_send(*all_parts)
    wait_send(*all_marks)
    for index in range(len(pieces)):
        wait_send(*forward_copy(index))
        wait_send(*back_copy(index))


def fused(predicted, observed, data_weight, bin_ids, offset_slots, conv_in, conv_mid, conv_out):
    traces, samples = predicted.shape
    owners = lax.axis_size("bin")
    group = traces // OFFS * (traces // owners)
    slots = owners * group
    pieces = gathered_pieces(samples)
    count = len(pieces)
    span = max(span_of(piece) for piece in pieces)
    cells = 2 * OFFS
    bf16 = jnp.bfloat16
    f32 = jnp.float32
    dma = pltpu.SemaphoreType.DMA
    vmem = pl.BlockSpec(memory_space=pltpu.VMEM)
    anywhere = pl.BlockSpec(memory_space=pl.ANY)

    def body(*refs):
        fused_body(owners, *refs)

    return pl.pallas_call(
        body,
        out_shape=jax.ShapeDtypeStruct((traces, samples), bf16),
        in_specs=[vmem, vmem, vmem, anywhere, anywhere, vmem, vmem, vmem],
        out_specs=vmem,
        scratch_shapes=[
            pltpu.VMEM((3 * OFFS, TILES * TILE), bf16),
            pltpu.VMEM((2, 4 * TILE, TILE), bf16),
            pltpu.VMEM((TILES * TILE, 3 * OFFS), bf16),
            pltpu.VMEM((slots, traces), bf16),
            pltpu.VMEM((slots, traces), bf16),
            pltpu.VMEM((slots, samples), bf16),
            pltpu.VMEM((slots, samples), bf16),
            pltpu.VMEM((slots, samples), bf16),
            pltpu.VMEM((slots, samples), bf16),
            pltpu.VMEM((traces, samples), f32),
            pltpu.VMEM((traces, samples), f32),
            pltpu.VMEM((traces, samples), f32),
            pltpu.VMEM((samples + 16, cells), f32),
            pltpu.VMEM(((span + 12) * BLK, cells), f32),
            pltpu.VMEM((2, (span + 14) * BLK, 3 * OFFS), bf16),
            pltpu.VMEM(((span + 14) * BLK, TILES * TILE), bf16),
            pltpu.VMEM((2, (span + 6) * BLK, 3 * OFFS), f32),
            pltpu.VMEM((span * BLK, cells), f32),
            pltpu.VMEM((8, 128), f32),
            pltpu.VMEM((8 * owners, 128), f32),
            dma((2,)),
            dma,
            dma,
            dma((count,)),
            dma((count,)),
            dma((count,)),
            dma((count,)),
            dma,
            dma,
        ],
        compiler_params=pltpu.CompilerParams(
            collective_id=0, has_side_effects=True, vmem_limit_bytes=53 * 1024 * 1024
        ),
        name="exchange_filter",
    )(
        predicted,
        bin_ids.reshape(1, traces),
        offset_slots.reshape(1, traces),
        observed,
        data_weight,
        conv_in,
        conv_mid.reshape(9 * CHAN, CHAN),
        conv_out,
    )


def local(*args):
    traces = args[0].shape[0]
    owners = lax.axis_size("bin")
    if traces // OFFS * (traces // owners) % 16 == 0:
        return fused(*args)
    return by_ops(*args)


def solution(mesh):
    in_specs = (
        P(("line", "bin"), None),
        P(("line", "bin"), None),
        P(("line", "bin"), None),
        P(("line", "bin")),
        P(("line", "bin")),
        P(),
        P(),
        P(),
    )
    out_specs = P(("line", "bin"), None)
    return jax.shard_map(local, mesh=mesh, in_specs=in_specs, out_specs=out_specs, check_vma=False)
```
